512 devices in a mesh: arm: 4 (over z_lo), gx: 8 (over x, core), gy: 16 (over y, z_hi).
Axes of the slice: x: 4, y: 4, z: 16 (z_hi: 4, z_lo: 4; z = z_hi * 4 + z_lo), core: 2. Of those that a mesh axis runs over, the one named last changes fastest.
Arguments:
- fields: float32 [4, 256, 256, 256], P('arm', 'gx', 'gy'), may hold values from -1.2 to 2
- flory_chi: float32 [4, 4], replicated, may hold values from 0 to 2
Outputs:
- field_out: float32 [4, 256, 256, 256], P('arm', 'gx', 'gy')
- volume_frac: float32 [4, 256, 256, 256], P('arm', 'gx', 'gy')
The draws below stay inside these ranges and needn't reach their ends.
All inputs are finite; a program needn't handle non-finite values.
Results may differ from the reference program's by a relative error of at most 0.0001.
Values sent between devices are 32-bit elements; how exact they have to be, the bound alone decides.
No kernel may reach another device: no remote copies, remote signals or barrier semaphores. Data moves between devices by JAX's collectives and lax.ppermute only.
A program may use at most 64 MiB of HBM per device.

```python
import jax
import jax.numpy as jnp

SPECIES = 4
STEPS = 8
NZ = 256
NX = 256
NY = 256


def draw_fields(key, part):
    first_key, second_key = jax.random.split(jax.random.fold_in(key, 17))
    x_frac = jnp.arange(NX, dtype=jnp.float32) / NX
    y_frac = jnp.arange(NY, dtype=jnp.float32) / NY
    rough = jax.random.uniform(first_key, (SPECIES, NX, NY, NZ), jnp.float32, -1.2, 1.2)
    ramp = 0.4 * (x_frac[:, None] + y_frac[None, :])
    scales = jax.random.uniform(second_key, (SPECIES,), jnp.float32, 0.5, 1.0)
    return rough + scales[:, None, None, None] * ramp[None, :, :, None]


def setup_inputs(seed: int = 0) -> dict:
    arg_keys = jax.random.split(jax.random.key(seed), 3)
    return {
        "fields": draw_fields(jax.random.fold_in(arg_keys[2], 71), 0),
        "flory_chi": jnp.clip(jax.random.uniform(arg_keys[1], (SPECIES, SPECIES), jnp.float32, 0.0, 2.0), 0.0, 2.0),
    }


diffusion = 0.14
contour_step = 0.05
mixing = 0.5
compress = 1.0


def laplace(field):
    spread = jnp.roll(field, 1, 0) + jnp.roll(field, -1, 0)
    spread = spread + jnp.roll(field, 1, 1) + jnp.roll(field, -1, 1)
    spread = spread + jnp.roll(field, 1, 2) + jnp.roll(field, -1, 2)
    return spread - 6.0 * field


def advance(state, field):
    return state + diffusion * laplace(state) - contour_step * field * state


def reference(fields, flory_chi):
    shape = fields.shape[1:]
    arm_ends = []
    for member in range(SPECIES):
        state = jnp.ones(shape, jnp.float32)
        for step_id in range(STEPS):
            state = advance(state, fields[member])
        arm_ends.append(state)
    junction_zero = arm_ends[1] * arm_ends[2]
    for other in range(3, SPECIES):
        junction_zero = junction_zero * arm_ends[other]
    mean_part = jnp.mean(junction_zero * arm_ends[0])
    volumes = []
    for member in range(SPECIES):
        junction = None
        for other in range(SPECIES):
            if other != member:
                junction = arm_ends[other] if junction is None else junction * arm_ends[other]
        state = jnp.ones(shape, jnp.float32)
        stored = [state]
        for step_id in range(STEPS):
            state = advance(state, fields[member])
            stored.append(state)
        outer = junction
        density = 0.5 * stored[STEPS] * outer
        for step_id in range(1, STEPS + 1):
            outer = advance(outer, fields[member])
            weight = 0.5 if step_id == STEPS else 1.0
            density = density + weight * stored[STEPS - step_id] * outer
        volumes.append(density / (SPECIES * STEPS * mean_part))
    pressure = compress * (sum(volumes) - 1.0)
    updated = []
    for member in range(SPECIES):
        mixture = flory_chi[member, 0] * volumes[0]
        for other in range(1, SPECIES):
            mixture = mixture + flory_chi[member, other] * volumes[other]
        field_new = fields[member] + mixing * (mixture + pressure - fields[member])
        updated.append(field_new - jnp.mean(field_new))
    return jnp.stack(updated), jnp.stack(volumes)
```

```python
import functools

import jax
import jax.numpy as jnp
from jax import lax
from jax.experimental import pallas as pl
from jax.experimental.pallas import tpu as pltpu
from jax.sharding import PartitionSpec as P

SPECIES = 4
STEPS = 8


diffusion = 0.14
contour_step = 0.05
mixing = 0.5
compress = 1.0

LANES = 128
COEF_ONE = (1.0 - 6.0 * diffusion) / diffusion
COEF_FIELD = contour_step / diffusion
SCALE = diffusion**STEPS

BX, BY = 32, 4
COEF_REACH = (6, 5, 4)
MID_REACH = (3, 2, 1, 0)
JUNC_REACH = (7, 6, 5, 4)


def packed_size(reach):
    return sum(BX + 2 * r for r in reach)


def lane_masks():
    lane = lax.broadcasted_iota(jnp.int32, (8, LANES), 1)
    return lane == LANES - 1, lane == 0


def step(src, dst, coef, xs, ys, coef_shift):
    y0, y1 = ys
    dx, dy = coef_shift
    last, first = lane_masks()

    @pl.loop(xs[0], xs[1])
    def _(x):
        v = src[x, y0:y1]
        other = pltpu.roll(v, 4, 1)
        up = pltpu.roll(jnp.where(last, other, v), 1, 2)
        down = pltpu.roll(jnp.where(first, other, v), LANES - 1, 2)
        total = (src[x - 1, y0:y1] + src[x + 1, y0:y1]) + (
            src[x, y0 - 1 : y1 - 1] + src[x, y0 + 1 : y1 + 1]
        )
        total = total + (up + down)
        dst[x, y0:y1] = total + coef[x + dx, y0 + dy : y1 + dy] * v


def interleave_kernel(recv, coef, sums):
    for s in range(SPECIES):
        part = recv[s]
        coef[pl.ds(s, 2 * BX * BY, stride=4), :] = COEF_ONE - COEF_FIELD * part
        sums[s : s + 1, :] = jnp.sum(part, axis=0, keepdims=True)
    sums[4:8, :] = jnp.zeros((4, LANES), jnp.float32)


def pack_kernel(reach, own, low, high, up, down):
    edge = low.shape[0]
    offset = 0
    for j, r in enumerate(reach):
        for dst, y in ((up, j), (down, BY - 1 - j)):
            dst[offset : offset + r] = low[edge - r : edge, y]
            dst[offset + r : offset + r + BX] = own[:, y]
            dst[offset + r + BX : offset + 2 * r + BX] = high[0:r, y]
        offset += BX + 2 * r


def unpack(dst, reach, low, high, shift):
    ox, oy = shift
    offset = 0
    for j, r in enumerate(reach):
        n = BX + 2 * r
        dst[ox - r : ox + BX + r, oy - 1 - j] = low[offset : offset + n]
        dst[ox - r : ox + BX + r, oy + BY + j] = high[offset : offset + n]
        offset += n


def emit(src, shift, reach, wide, up, down):
    ox, oy = shift
    wide[...] = src[ox - 4 : ox + BX + 4, oy : oy + BY]
    offset = 0
    for j, r in enumerate(reach):
        n = BX + 2 * r
        up[offset : offset + n] = src[ox - r : ox + BX + r, oy + j]
        down[offset : offset + n] = src[ox - r : ox + BX + r, oy + BY - 1 - j]
        offset += n


def inner_first(own, xlow, xhigh, ylow, yhigh, coef, s2, s3, wide, up, down, a, b):
    coef[7 : 7 + BX, 3:7] = own[...]
    coef[0:7, 3:7] = xlow[...]
    coef[7 + BX :, 3:7] = xhigh[...]
    unpack(coef, COEF_REACH, ylow, yhigh, (7, 3))
    here = (slice(7, 7 + BX), slice(3, 7))

    @pl.loop(0, 14 + BX)
    def _(x):
        a[x] = 6.0 + coef[x]

    step(a, b, coef, (1, 45), (1, 9), (0, 0))
    s2[...] = b[here]
    step(b, a, coef, (2, 44), (2, 8), (0, 0))
    s3[...] = a[here]
    step(a, b, coef, (3, 43), (3, 7), (0, 0))
    emit(b, (7, 3), MID_REACH, wide, up, down)


def others(v, shift):
    row = lax.broadcasted_iota(jnp.int32, (8, LANES), 0) % 4
    return jnp.where(
        row + shift < 4, pltpu.roll(v, 8 - shift, 1), pltpu.roll(v, 4 - shift, 1)
    )


def inner_second(wide, ylow, yhigh, coef, s5, s6, s7, s8, junction, part, a, b):
    a[0 : BX + 8, 4:8] = wide[...]
    unpack(a, MID_REACH, ylow, yhigh, (4, 4))
    here = (slice(4, 4 + BX), slice(4, 8))
    step(a, b, coef, (1, 39), (1, 11), (3, -1))
    s5[...] = b[here]
    step(b, a, coef, (2, 38), (2, 10), (3, -1))
    s6[...] = a[here]
    step(a, b, coef, (3, 37), (3, 9), (3, -1))
    s7[...] = b[here]
    step(b, a, coef, (4, 36), (4, 8), (3, -1))
    part[...] = jnp.zeros_like(part)

    @pl.loop(0, BX)
    def _(x):
        q = a[x + 4, 4:8]
        s8[x] = q
        true = q * SCALE
        product = others(true, 1) * others(true, 2) * others(true, 3)
        junction[x] = product
        part[...] += jnp.sum(q * product, axis=0)


def outer_first(
    own, xlow, xhigh, ylow, yhigh, coef, s4, s5, s6, s7, s8, dens, wide, up, down, a, b
):
    a[8 : 8 + BX, 4:8] = own[...]
    a[0:8, 4:8] = xlow[...]
    a[8 + BX :, 4:8] = xhigh[...]
    unpack(a, JUNC_REACH, ylow, yhigh, (8, 4))
    here = (slice(8, 8 + BX), slice(4, 8))
    shift = (-1, -1)
    dens[...] = 0.5 * s8[...] * own[...]
    step(a, b, coef, (1, 47), (1, 11), shift)
    dens[...] += s7[...] * b[here]
    step(b, a, coef, (2, 46), (2, 10), shift)
    dens[...] += s6[...] * a[here]
    step(a, b, coef, (3, 45), (3, 9), shift)
    dens[...] += s5[...] * b[here]
    step(b, a, coef, (4, 44), (4, 8), shift)
    dens[...] += s4[4 : 4 + BX] * a[here]
    emit(a, (8, 4), MID_REACH, wide, up, down)


def outer_second(wide, ylow, yhigh, coef, s2, s3, dens, mix, out, a, b, flat):
    a[0 : BX + 8, 4:8] = wide[...]
    unpack(a, MID_REACH, ylow, yhigh, (4, 4))
    here = (slice(4, 4 + BX), slice(4, 8))
    step(a, b, coef, (1, 39), (1, 11), (3, -1))
    d5 = (here, b)
    dens_now = dens[...] + s3[...] * b[here]
    a_prev = dens_now
    flat[0] = a_prev.reshape(8 * BX * BY, LANES)
    step(b, a, coef, (2, 38), (2, 10), (3, -1))
    flat[0] = flat[0] + (s2[...] * a[here]).reshape(8 * BX * BY, LANES)
    step(a, b, coef, (3, 37), (3, 9), (3, -1))
    s1 = 6.0 + coef[7 : 7 + BX, 3:7]
    flat[0] = flat[0] + (s1 * b[here]).reshape(8 * BX * BY, LANES)
    step(b, a, coef, (4, 36), (4, 8), (3, -1))
    flat[0] = flat[0] + (0.5 * a[here]).reshape(8 * BX * BY, LANES)

    @pl.loop(0, BX)
    def _(x):
        rows = pl.ds(pl.multiple_of(x * 8 * BY, 8 * BY), 8 * BY)
        d = flat[0, rows].reshape(BY, 8, LANES)
        mixed = mix[0] * d
        for k in range(1, SPECIES):
            mixed = mixed + mix[k] * others(d, k)
        flat[1, rows] = mixed.reshape(8 * BY, LANES)

    n = 2 * BX * BY
    for s in range(SPECIES):
        for i in range(2):
            out[s, i * n : (i + 1) * n, :] = flat[i, pl.ds(s, n, stride=4), :]


def tiles(*lead):
    return jax.ShapeDtypeStruct(lead + (8, LANES), jnp.float32)


def scratch(*lead):
    return pltpu.VMEM(lead + (8, LANES), jnp.float32)


def call(kernel, outs, scratches=()):
    return pl.pallas_call(
        kernel,
        out_shape=outs,
        scratch_shapes=list(scratches),
        compiler_params=pltpu.CompilerParams(vmem_limit_bytes=40 * 1024 * 1024),
    )


def local(fields, flory_chi):
    field_here = fields[0]
    arm_index = lax.axis_index("arm")
    arms, size_gx, size_gy = (lax.axis_size(a) for a in ("arm", "gx", "gy"))
    size_z = field_here.shape[2]
    cell_count = BX * 16 * size_z * size_gx * size_gy

    def ring(shift):
        size = arms * size_gy
        at = lambda r: (r % arms) * size_gy + (r % size) // arms
        return [(at(r), at(r + shift)) for r in range(size)]

    def along_y(up, down):
        low = lax.ppermute(down, ("arm", "gy"), ring(1))
        high = lax.ppermute(up, ("arm", "gy"), ring(-1 + arms * size_gy))
        return low, high

    def along_x(array, width):
        n = size_gx
        low = lax.ppermute(array[BX - width :], "gx", [(i, (i + 1) % n) for i in range(n)])
        high = lax.ppermute(array[:width], "gx", [(i, (i - 1) % n) for i in range(n)])
        return low, high

    def pack(reach, own, low, high):
        size = packed_size(reach)
        return call(functools.partial(pack_kernel, reach), (tiles(size),) * 2)(own, low, high)

    payload = field_here.reshape(BX, arms, BY, 2, LANES).transpose(1, 0, 2, 3, 4)
    payload = payload.reshape(arms, 2 * BX * BY, LANES)
    recv = lax.all_to_all(payload, "arm", 0, 0)
    coef_flat, field_sums = call(
        interleave_kernel,
        (jax.ShapeDtypeStruct((8 * BX * BY, LANES), jnp.float32), tiles()),
    )(recv)
    coef_own = coef_flat.reshape(BX, BY, 8, LANES)
    xlow, xhigh = along_x(coef_own, 7)
    ylow, yhigh = along_y(*pack(COEF_REACH, coef_own, xlow[:], xhigh[:]))

    own = tiles(BX, BY)
    mid = packed_size(MID_REACH)
    coef, s2, s3, s4, up, down = call(
        inner_first,
        (tiles(14 + BX, 6 + BY), own, own, tiles(BX + 8, BY), tiles(mid), tiles(mid)),
        [scratch(14 + BX, 6 + BY)] * 2,
    )(coef_own, xlow, xhigh, ylow, yhigh)
    ylow, yhigh = along_y(up, down)
    s5, s6, s7, s8, junction, part = call(
        inner_second, (own,) * 5 + (tiles(),), [scratch(BX + 8, BY + 8)] * 2
    )(s4, ylow, yhigh, coef)

    sums = jnp.stack([part, field_sums])
    sums = jnp.sum(
        lax.all_to_all(jnp.broadcast_to(sums, (size_gx,) + sums.shape), "gx", 0, 0), axis=0
    )
    sums = jnp.sum(
        lax.all_to_all(jnp.broadcast_to(sums, (size_gy,) + sums.shape), "gy", 0, 0), axis=0
    )

    xlow, xhigh = along_x(junction, 8)
    ylow, yhigh = along_y(*pack(JUNC_REACH, junction, xlow, xhigh))
    dens, wide, up, down = call(
        outer_first,
        (own, tiles(BX + 8, BY), tiles(mid), tiles(mid)),
        [scratch(16 + BX, 8 + BY)] * 2,
    )(junction, xlow, xhigh, ylow, yhigh, coef, s4, s5, s6, s7, s8)
    ylow, yhigh = along_y(up, down)

    weights = flory_chi + compress
    mix = jnp.stack(
        [
            jnp.tile(jnp.stack([weights[a, (a + k) % SPECIES] for a in range(SPECIES)]), 2)
            for k in range(SPECIES)
        ]
    )
    mix = jnp.broadcast_to(mix[:, :, None], (SPECIES, 8, LANES))
    out = call(
        outer_second,
        jax.ShapeDtypeStruct((arms, 4 * BX * BY, LANES), jnp.float32),
        [scratch(BX + 8, BY + 8)] * 2 + [pltpu.VMEM((2, 8 * BX * BY, LANES), jnp.float32)],
    )(wide, ylow, yhigh, coef, s2, s3, dens, mix)

    tail = jnp.broadcast_to(sums.reshape(1, 16, LANES), (arms, 16, LANES))
    back = lax.all_to_all(jnp.concatenate([out, tail], axis=1), "arm", 0, 0)
    totals = jnp.sum(back[:, 4 * BX * BY :], axis=0)
    chain = jnp.sum(totals[:8]) / SPECIES
    field_sum = jnp.sum(
        jnp.where((jnp.arange(8) == arm_index)[:, None], totals[8:], 0.0)
    )
    scale = cell_count / (SPECIES * STEPS * chain)

    def unfold(flat):
        flat = flat.reshape(arms, BX, BY, 2, LANES).transpose(1, 0, 2, 3, 4)
        return flat.reshape(field_here.shape)

    n = 2 * BX * BY
    volume = unfold(back[:, :n]) * scale
    mixture = unfold(back[:, n : 2 * n]) * scale
    chi_sum = jnp.sum(
        jnp.where((jnp.arange(SPECIES) == arm_index)[:, None], flory_chi, 0.0)
    )
    mean_new = (1.0 - mixing) * field_sum / cell_count + mixing * chi_sum / SPECIES
    field_new = field_here + mixing * (mixture - compress - field_here)
    field_out = field_new - mean_new
    return (field_out[None], volume[None])


def solution(mesh):
    placed = (P("arm", "gx", "gy", None), P())
    return jax.shard_map(
        local,
        mesh=mesh,
        in_specs=placed,
        out_specs=(P("arm", "gx", "gy", None), P("arm", "gx", "gy", None)),
        check_vma=False,
    )
```

```python
import functools

import jax
import jax.numpy as jnp
from jax import lax
from jax.experimental import pallas as pl
from jax.experimental.pallas import tpu as pltpu
from jax.sharding import PartitionSpec as P

SPECIES = 4
STEPS = 8


diffusion = 0.14
contour_step = 0.05
mixing = 0.5
compress = 1.0

LANES = 128
COEF_ONE = (1.0 - 6.0 * diffusion) / diffusion
COEF_FIELD = contour_step / diffusion
SCALE = diffusion**STEPS

BX, BY = 32, 4
VMEM_LIMIT = 16 * 1024 * 1024
COEF_REACH = (6, 5, 4)
MID_REACH = (3, 2, 1, 0)
JUNC_REACH = (7, 6, 5, 4)


def packed_size(reach):
    return sum(BX + 2 * r for r in reach)


def lane_masks():
    lane = lax.broadcasted_iota(jnp.int32, (8, LANES), 1)
    return lane == LANES - 1, lane == 0


def step(src, dst, coef, xs, ys, coef_shift):
    (x0, x1), (y0, y1) = xs, ys
    dx, dy = coef_shift
    last, first = lane_masks()
    v = src[x0:x1, y0:y1]
    other = pltpu.roll(v, 4, 2)
    up = pltpu.roll(jnp.where(last, other, v), 1, 3)
    down = pltpu.roll(jnp.where(first, other, v), LANES - 1, 3)
    total = (src[x0 - 1 : x1 - 1, y0:y1] + src[x0 + 1 : x1 + 1, y0:y1]) + (
        src[x0:x1, y0 - 1 : y1 - 1] + src[x0:x1, y0 + 1 : y1 + 1]
    )
    dst[x0:x1, y0:y1] = total + (up + down) + coef[x0 + dx : x1 + dx, y0 + dy : y1 + dy] * v


def interleave_kernel(recv, coef, sums):
    n = BX * BY
    for s in range(SPECIES):
        for half in range(2):
            coef[pl.ds(half * 4 + s, n, stride=8), :] = (
                COEF_ONE - COEF_FIELD * recv[s, half * n : (half + 1) * n]
            )
        sums[s : s + 1, :] = jnp.sum(recv[s], axis=0, keepdims=True)
    sums[4:8, :] = jnp.zeros((4, LANES), jnp.float32)


def by_side(arm, first, second, body):
    odd = arm[0] % 2

    @pl.when(odd == 0)
    def _():
        body(second, first)

    @pl.when(odd == 1)
    def _():
        body(first, second)


def pack_kernel(reach, arm, own, low, high, first, second):
    edge = low.shape[0]

    def body(up, down):
        offset = 0
        for j, r in enumerate(reach):
            for dst, y in ((up, j), (down, BY - 1 - j)):
                dst[offset : offset + r] = low[edge - r : edge, y]
                dst[offset + r : offset + r + BX] = own[:, y]
                dst[offset + r + BX : offset + 2 * r + BX] = high[0:r, y]
            offset += BX + 2 * r

    by_side(arm, first, second, body)


def unpack(arm, dst, reach, first, second, shift):
    ox, oy = shift

    def body(low, high):
        offset = 0
        for j, r in enumerate(reach):
            n = BX + 2 * r
            dst[ox - r : ox + BX + r, oy - 1 - j] = low[offset : offset + n]
            dst[ox - r : ox + BX + r, oy + BY + j] = high[offset : offset + n]
            offset += n

    by_side(arm, first, second, body)


def emit(arm, src, shift, reach, wide, first, second):
    ox, oy = shift
    wide[...] = src[ox - 4 : ox + BX + 4, oy : oy + BY]

    def body(up, down):
        offset = 0
        for j, r in enumerate(reach):
            n = BX + 2 * r
            up[offset : offset + n] = src[ox - r : ox + BX + r, oy + j]
            down[offset : offset + n] = src[ox - r : ox + BX + r, oy + BY - 1 - j]
            offset += n

    by_side(arm, first, second, body)


def inner_first(arm, own, xlow, xhigh, y1, y2, coef, s2, s3, wide, e1, e2, a, b):
    coef[7 : 7 + BX, 3:7] = own[...]
    coef[0:7, 3:7] = xlow[...]
    coef[7 + BX :, 3:7] = xhigh[...]
    unpack(arm, coef, COEF_REACH, y1, y2, (7, 3))
    here = (slice(7, 7 + BX), slice(3, 7))
    a[...] = 6.0 + coef[...]
    step(a, b, coef, (1, 45), (1, 9), (0, 0))
    s2[...] = b[here]
    step(b, a, coef, (2, 44), (2, 8), (0, 0))
    s3[...] = a[here]
    step(a, b, coef, (3, 43), (3, 7), (0, 0))
    emit(arm, b, (7, 3), MID_REACH, wide, e1, e2)


def others(v, shift):
    axis = v.ndim - 2
    row = lax.broadcasted_iota(jnp.int32, (8, LANES), 0) % 4
    return jnp.where(
        row + shift < 4, pltpu.roll(v, 8 - shift, axis), pltpu.roll(v, 4 - shift, axis)
    )


def inner_second(
    arm, wide, y1, y2, coef, sums, s5, s6, s7, s8, junction, spread, a, b
):
    a[0 : BX + 8, 4:8] = wide[...]
    unpack(arm, a, MID_REACH, y1, y2, (4, 4))
    here = (slice(4, 4 + BX), slice(4, 8))
    step(a, b, coef, (1, 39), (1, 11), (3, -1))
    s5[...] = b[here]
    step(b, a, coef, (2, 38), (2, 10), (3, -1))
    s6[...] = a[here]
    step(a, b, coef, (3, 37), (3, 9), (3, -1))
    s7[...] = b[here]
    step(b, a, coef, (4, 36), (4, 8), (3, -1))
    part = jnp.zeros((8, LANES), jnp.float32)
    for x in range(BX):
        q = a[x + 4, 4:8]
        s8[x] = q
        true = q * SCALE
        product = others(true, 1) * others(true, 2) * others(true, 3)
        junction[x] = product
        part = part + jnp.sum(q * product, axis=0)
    row = lax.broadcasted_iota(jnp.int32, (8, LANES), 0)
    chain = jnp.broadcast_to(jnp.sum(part, axis=0, keepdims=True), (8, LANES))
    spread[...] = jnp.broadcast_to(jnp.where(row == 4, chain, sums[...]), spread.shape)


def outer_first(
    arm, own, xlow, xhigh, y1, y2, coef, s4, s5, s6, s7, s8, got,
    dens, wide, e1, e2, spread, a, b
):
    spread[...] = jnp.broadcast_to(jnp.sum(got[...], axis=0), spread.shape)
    a[8 : 8 + BX, 4:8] = own[...]
    a[0:8, 4:8] = xlow[...]
    a[8 + BX :, 4:8] = xhigh[...]
    unpack(arm, a, JUNC_REACH, y1, y2, (8, 4))
    here = (slice(8, 8 + BX), slice(4, 8))
    shift = (-1, -1)
    step(a, b, coef, (1, 47), (1, 11), shift)
    dens[...] = 0.5 * s8[...] * own[...] + s7[...] * b[here]
    step(b, a, coef, (2, 46), (2, 10), shift)
    dens[...] += s6[...] * a[here]
    step(a, b, coef, (3, 45), (3, 9), shift)
    dens[...] += s5[...] * b[here]
    step(b, a, coef, (4, 44), (4, 8), shift)
    dens[...] += s4[4 : 4 + BX] * a[here]
    emit(arm, a, (8, 4), MID_REACH, wide, e1, e2)


def outer_second(
    arm, chi, wide, y1, y2, coef, s2, s3, dens, got, out, a, b, flat, mixed
):
    a[0 : BX + 8, 4:8] = wide[...]
    unpack(arm, a, MID_REACH, y1, y2, (4, 4))
    here = (slice(4, 4 + BX), slice(4, 8))
    rows = (8 * BX * BY, LANES)
    step(a, b, coef, (1, 39), (1, 11), (3, -1))
    flat[...] = (dens[...] + s3[...] * b[here]).reshape(rows)
    step(b, a, coef, (2, 38), (2, 10), (3, -1))
    flat[...] += (s2[...] * a[here]).reshape(rows)
    step(a, b, coef, (3, 37), (3, 9), (3, -1))
    flat[...] += ((6.0 + coef[7 : 7 + BX, 3:7]) * b[here]).reshape(rows)
    step(b, a, coef, (4, 36), (4, 8), (3, -1))
    d = flat[...].reshape(BX, BY, 8, LANES) + 0.5 * a[here]
    flat[...] = d.reshape(rows)
    row = lax.broadcasted_iota(jnp.int32, (8, LANES), 0) % 4
    total = None
    for k in range(SPECIES):
        weight = jnp.zeros((8, LANES), jnp.float32)
        for s in range(SPECIES):
            weight = jnp.where(row == s, chi[s, (s + k) % SPECIES] + compress, weight)
        term = weight * (others(d, k) if k else d)
        total = term if total is None else total + term
    mixed[...] = total.reshape(rows)
    n = BX * BY
    tail = jnp.sum(got[...], axis=0)
    for s in range(SPECIES):
        for i, src in enumerate((flat, mixed)):
            for half in range(2):
                at = (2 * i + half) * n
                out[s, at : at + n, :] = src[pl.ds(half * 4 + s, n, stride=8), :]
        out[s, 4 * n : 4 * n + 8, :] = tail


def finish(cell_count, arm, chi, back, field, new, volume):
    n = BX * BY
    here = arm[0]
    tail = jnp.sum(back[:, 4 * n : 4 * n + 8], axis=0)
    row = lax.broadcasted_iota(jnp.int32, (8, LANES), 0)
    chain = jnp.sum(jnp.where(row == 4, tail, 0.0), keepdims=True) / SPECIES
    field_sum = jnp.sum(jnp.where(row == here, tail, 0.0), keepdims=True)
    scale = cell_count / (SPECIES * STEPS * chain)
    chi_sum = chi[here, 0]
    for s in range(1, SPECIES):
        chi_sum = chi_sum + chi[here, s]
    mean_new = (1.0 - mixing) / cell_count * field_sum + mixing * chi_sum / SPECIES
    for q in range(SPECIES):
        for half in range(2):
            lanes = slice(half * LANES, (half + 1) * LANES)
            for x in range(BX):
                at = half * n + x * BY
                ys = slice(q * BY, (q + 1) * BY)
                volume[x, ys, lanes] = scale * back[q, at : at + BY, :]
                mixture = scale * back[q, 2 * n + at : 2 * n + at + BY, :]
                old = field[x, ys, lanes]
                new[x, ys, lanes] = old + mixing * (mixture - compress - old) - mean_new


def tiles(*lead):
    return jax.ShapeDtypeStruct(lead + (8, LANES), jnp.float32)


def scratch(*lead):
    return pltpu.VMEM(lead + (8, LANES), jnp.float32)


def call(kernel, outs, scratches=(), scalars=0, arrays=0):
    in_specs = [pl.BlockSpec(memory_space=pltpu.SMEM)] * scalars
    in_specs += [pl.BlockSpec(memory_space=pltpu.VMEM)] * arrays
    return pl.pallas_call(
        kernel,
        out_shape=outs,
        in_specs=in_specs,
        scratch_shapes=list(scratches),
        compiler_params=pltpu.CompilerParams(vmem_limit_bytes=VMEM_LIMIT),
    )


def local(fields, flory_chi):
    field_here = fields[0]
    arm = lax.axis_index("arm")[None]
    arms, size_gx, size_gy = (lax.axis_size(a) for a in ("arm", "gx", "gy"))
    cell_count = field_here.size * size_gx * size_gy
    n = BX * BY

    size = arms * size_gy
    at = lambda r: (r % arms) * size_gy + (r % size) // arms
    first_pairs = [(at(r), at(r ^ 1)) for r in range(size)]
    second_pairs = [(at(r), at(((r + 1) ^ 1) - 1)) for r in range(size)]

    def along_y(first, second):
        return (
            lax.ppermute(first, ("arm", "gy"), first_pairs),
            lax.ppermute(second, ("arm", "gy"), second_pairs),
        )

    def along_x(array, width):
        m = size_gx
        low = lax.ppermute(array[BX - width :], "gx", [(i, (i + 1) % m) for i in range(m)])
        high = lax.ppermute(array[:width], "gx", [(i, (i - 1) % m) for i in range(m)])
        return low, high

    def pack(reach, own, low, high):
        kernel = functools.partial(pack_kernel, reach)
        outs = (tiles(packed_size(reach)),) * 2
        return call(kernel, outs, scalars=1, arrays=3)(arm, own, low, high)

    payload = field_here.reshape(BX, arms, BY, 2, LANES).transpose(1, 3, 0, 2, 4)
    recv = lax.all_to_all(payload.reshape(arms, 2 * n, LANES), "arm", 0, 0)
    coef_flat, sums = call(
        interleave_kernel,
        (jax.ShapeDtypeStruct((8 * n, LANES), jnp.float32), tiles()),
        arrays=1,
    )(recv)
    coef_own = coef_flat.reshape(BX, BY, 8, LANES)
    xlow, xhigh = along_x(coef_own, 7)
    y1, y2 = along_y(*pack(COEF_REACH, coef_own, xlow, xhigh))

    own, wide_shape = tiles(BX, BY), tiles(BX + 8, BY)
    mid = tiles(packed_size(MID_REACH))
    coef, s2, s3, s4, e1, e2 = call(
        inner_first,
        (tiles(14 + BX, 6 + BY), own, own, wide_shape, mid, mid),
        [scratch(14 + BX, 6 + BY)] * 2,
        scalars=1,
        arrays=5,
    )(arm, coef_own, xlow, xhigh, y1, y2)
    y1, y2 = along_y(e1, e2)
    s5, s6, s7, s8, junction, spread = call(
        inner_second,
        (own,) * 5 + (tiles(size_gy),),
        [scratch(BX + 8, BY + 8)] * 2,
        scalars=1,
        arrays=5,
    )(arm, s4, y1, y2, coef, sums)

    got = lax.all_to_all(spread, "gy", 0, 0)
    xlow, xhigh = along_x(junction, 8)
    y1, y2 = along_y(*pack(JUNC_REACH, junction, xlow, xhigh))
    dens, wide, e1, e2, spread = call(
        outer_first,
        (own, wide_shape, mid, mid, tiles(size_gx)),
        [scratch(16 + BX, 8 + BY)] * 2,
        scalars=1,
        arrays=12,
    )(arm, junction, xlow, xhigh, y1, y2, coef, s4, s5, s6, s7, s8, got)
    got = lax.all_to_all(spread, "gx", 0, 0)
    y1, y2 = along_y(e1, e2)
    out = call(
        outer_second,
        jax.ShapeDtypeStruct((arms, 4 * n + 8, LANES), jnp.float32),
        [scratch(BX + 8, BY + 8)] * 2 + [pltpu.VMEM((8 * n, LANES), jnp.float32)] * 2,
        scalars=2,
        arrays=8,
    )(arm, flory_chi, wide, y1, y2, coef, s2, s3, dens, got)

    back = lax.all_to_all(out, "arm", 0, 0)
    result = jax.ShapeDtypeStruct(field_here.shape, jnp.float32)
    field_out, volume = call(
        functools.partial(finish, cell_count), (result, result), scalars=2, arrays=2
    )(arm, flory_chi, back, field_here)
    return (field_out[None], volume[None])


def solution(mesh):
    placed = (P("arm", "gx", "gy", None), P())
    return jax.shard_map(
        local,
        mesh=mesh,
        in_specs=placed,
        out_specs=(P("arm", "gx", "gy", None), P("arm", "gx", "gy", None)),
        check_vma=False,
    )
```

```python
import functools

import jax
import jax.numpy as jnp
from jax import lax
from jax.experimental import pallas as pl
from jax.experimental.pallas import tpu as pltpu
from jax.sharding import PartitionSpec as P

SPECIES = 4
STEPS = 8


diffusion = 0.14
contour_step = 0.05
mixing = 0.5
compress = 1.0

LANES = 128
COEF_ONE = (1.0 - 6.0 * diffusion) / diffusion
COEF_FIELD = contour_step / diffusion
SCALE = diffusion**STEPS

BX, BY = 32, 4
VMEM_LIMIT = 16 * 1024 * 1024
COEF_REACH = (6, 5, 4)
MID_REACH = (3, 2, 1, 0)
JUNC_REACH = (7, 6, 5, 4)


def packed_size(reach):
    return sum(BX + 2 * r for r in reach)


def side_size(reach):
    return BY * (reach[0] + 1) + 2 * sum(reach)


def lane_masks():
    lane = lax.broadcasted_iota(jnp.int32, (8, LANES), 1)
    return lane == LANES - 1, lane == 0


def step(src, dst, coef, xs, ys, coef_shift):
    (x0, x1), (y0, y1) = xs, ys
    dx, dy = coef_shift
    last, first = lane_masks()
    v = src[x0:x1, y0:y1]
    other = pltpu.roll(v, 4, 2)
    up = pltpu.roll(jnp.where(last, other, v), 1, 3)
    down = pltpu.roll(jnp.where(first, other, v), LANES - 1, 3)
    total = (src[x0 - 1 : x1 - 1, y0:y1] + src[x0 + 1 : x1 + 1, y0:y1]) + (
        src[x0:x1, y0 - 1 : y1 - 1] + src[x0:x1, y0 + 1 : y1 + 1]
    )
    dst[x0:x1, y0:y1] = total + (up + down) + coef[x0 + dx : x1 + dx, y0 + dy : y1 + dy] * v


def interleave_kernel(arm, recv, coef, sums, first, second):
    n = BX * BY
    for s in range(SPECIES):
        for half in range(2):
            coef[pl.ds(half * 4 + s, n, stride=8), :] = (
                COEF_ONE - COEF_FIELD * recv[s, half * n : (half + 1) * n]
            )
        sums[s : s + 1, :] = jnp.sum(recv[s], axis=0, keepdims=True)
    sums[4:8, :] = jnp.zeros((4, LANES), jnp.float32)

    def body(up, down):
        cells = coef[...].reshape(BX, BY, 8, LANES)
        for j in range(len(COEF_REACH)):
            up[:, j] = cells[:, j]
            down[:, BY - 2 - j] = cells[:, BY - 1 - j]

    by_side(arm, first, second, body)


def by_side(arm, first, second, body):
    odd = arm[0] % 2

    @pl.when(odd == 0)
    def _():
        body(second, first)

    @pl.when(odd == 1)
    def _():
        body(first, second)


def pack_sides(reach, arm, own, first, second, *rest):
    if len(rest) == 4:
        got, left, right, spread = rest
        spread[...] = jnp.broadcast_to(jnp.sum(got[...], axis=0), spread.shape)
    else:
        left, right = rest
    width, depth = reach[0] + 1, len(reach)

    def put(at, src, y, r):
        left[at : at + r] = src[0:r, y]
        right[at : at + r] = src[BX - r : BX, y]
        return at + r

    def body(low, high):
        at = 0
        for y in range(BY):
            at = put(at, own, y, width)
        for j, r in enumerate(reach):
            at = put(at, low, depth - 1 - j, r)
            at = put(at, high, j, r)

    by_side(arm, first, second, body)


def surround(arm, dst, reach, own, first, second, xlow, xhigh, shift):
    ox, oy = shift
    width, depth = reach[0] + 1, len(reach)
    dst[ox : ox + BX, oy : oy + BY] = own[...]

    def put(at, y, r):
        dst[ox - r : ox, y] = xlow[at : at + r]
        dst[ox + BX : ox + BX + r, y] = xhigh[at : at + r]
        return at + r

    at = 0
    for y in range(BY):
        at = put(at, oy + y, width)
    for j, r in enumerate(reach):
        at = put(at, oy - 1 - j, r)
        at = put(at, oy + BY + j, r)

    def body(low, high):
        dst[ox : ox + BX, oy - depth : oy] = low[...]
        dst[ox : ox + BX, oy + BY : oy + BY + depth] = high[...]

    by_side(arm, first, second, body)


def unpack(arm, dst, reach, first, second, shift):
    ox, oy = shift

    def body(low, high):
        offset = 0
        for j, r in enumerate(reach):
            n = BX + 2 * r
            dst[ox - r : ox + BX + r, oy - 1 - j] = low[offset : offset + n]
            dst[ox - r : ox + BX + r, oy + BY + j] = high[offset : offset + n]
            offset += n

    by_side(arm, first, second, body)


def emit(arm, src, shift, reach, wide, first, second):
    ox, oy = shift
    wide[...] = src[ox - 4 : ox + BX + 4, oy : oy + BY]

    def body(up, down):
        offset = 0
        for j, r in enumerate(reach):
            n = BX + 2 * r
            up[offset : offset + n] = src[ox - r : ox + BX + r, oy + j]
            down[offset : offset + n] = src[ox - r : ox + BX + r, oy + BY - 1 - j]
            offset += n

    by_side(arm, first, second, body)


def inner_first(arm, own, xlow, xhigh, y1, y2, coef, s2, s3, wide, e1, e2, a, b):
    surround(arm, coef, COEF_REACH, own, y1, y2, xlow, xhigh, (7, 3))
    here = (slice(7, 7 + BX), slice(3, 7))
    a[...] = 6.0 + coef[...]
    step(a, b, coef, (1, 45), (1, 9), (0, 0))
    s2[...] = b[here]
    step(b, a, coef, (2, 44), (2, 8), (0, 0))
    s3[...] = a[here]
    step(a, b, coef, (3, 43), (3, 7), (0, 0))
    emit(arm, b, (7, 3), MID_REACH, wide, e1, e2)


def others(v, shift):
    axis = v.ndim - 2
    row = lax.broadcasted_iota(jnp.int32, (8, LANES), 0) % 4
    return jnp.where(
        row + shift < 4, pltpu.roll(v, 8 - shift, axis), pltpu.roll(v, 4 - shift, axis)
    )


def inner_second(
    arm, wide, y1, y2, coef, sums, s5, s6, s7, s8, junction, spread, a, b
):
    a[0 : BX + 8, 4:8] = wide[...]
    unpack(arm, a, MID_REACH, y1, y2, (4, 4))
    here = (slice(4, 4 + BX), slice(4, 8))
    step(a, b, coef, (1, 39), (1, 11), (3, -1))
    s5[...] = b[here]
    step(b, a, coef, (2, 38), (2, 10), (3, -1))
    s6[...] = a[here]
    step(a, b, coef, (3, 37), (3, 9), (3, -1))
    s7[...] = b[here]
    step(b, a, coef, (4, 36), (4, 8), (3, -1))
    part = jnp.zeros((8, LANES), jnp.float32)
    for x in range(BX):
        q = a[x + 4, 4:8]
        s8[x] = q
        true = q * SCALE
        product = others(true, 1) * others(true, 2) * others(true, 3)
        junction[x] = product
        part = part + jnp.sum(q * product, axis=0)
    row = lax.broadcasted_iota(jnp.int32, (8, LANES), 0)
    chain = jnp.broadcast_to(jnp.sum(part, axis=0, keepdims=True), (8, LANES))
    spread[...] = jnp.broadcast_to(jnp.where(row == 4, chain, sums[...]), spread.shape)


def outer_first(
    arm, own, xlow, xhigh, y1, y2, coef, s4, s5, s6, s7, s8, got,
    dens, wide, e1, e2, spread, a, b
):
    spread[...] = jnp.broadcast_to(jnp.sum(got[...], axis=0), spread.shape)
    surround(arm, a, JUNC_REACH, own, y1, y2, xlow, xhigh, (8, 4))
    here = (slice(8, 8 + BX), slice(4, 8))
    shift = (-1, -1)
    step(a, b, coef, (1, 47), (1, 11), shift)
    dens[...] = 0.5 * s8[...] * own[...] + s7[...] * b[here]
    step(b, a, coef, (2, 46), (2, 10), shift)
    dens[...] += s6[...] * a[here]
    step(a, b, coef, (3, 45), (3, 9), shift)
    dens[...] += s5[...] * b[here]
    step(b, a, coef, (4, 44), (4, 8), shift)
    dens[...] += s4[4 : 4 + BX] * a[here]
    emit(arm, a, (8, 4), MID_REACH, wide, e1, e2)


def outer_second(
    arm, chi, wide, y1, y2, coef, s2, s3, dens, got, out, a, b, flat, mixed
):
    a[0 : BX + 8, 4:8] = wide[...]
    unpack(arm, a, MID_REACH, y1, y2, (4, 4))
    here = (slice(4, 4 + BX), slice(4, 8))
    rows = (8 * BX * BY, LANES)
    step(a, b, coef, (1, 39), (1, 11), (3, -1))
    flat[...] = (dens[...] + s3[...] * b[here]).reshape(rows)
    step(b, a, coef, (2, 38), (2, 10), (3, -1))
    flat[...] += (s2[...] * a[here]).reshape(rows)
    step(a, b, coef, (3, 37), (3, 9), (3, -1))
    flat[...] += ((6.0 + coef[7 : 7 + BX, 3:7]) * b[here]).reshape(rows)
    step(b, a, coef, (4, 36), (4, 8), (3, -1))
    d = flat[...].reshape(BX, BY, 8, LANES) + 0.5 * a[here]
    flat[...] = d.reshape(rows)
    row = lax.broadcasted_iota(jnp.int32, (8, LANES), 0) % 4
    total = None
    for k in range(SPECIES):
        weight = jnp.zeros((8, LANES), jnp.float32)
        for s in range(SPECIES):
            weight = jnp.where(row == s, chi[s, (s + k) % SPECIES] + compress, weight)
        term = weight * (others(d, k) if k else d)
        total = term if total is None else total + term
    mixed[...] = total.reshape(rows)
    n = BX * BY
    tail = jnp.sum(got[...], axis=0)
    for s in range(SPECIES):
        for i, src in enumerate((flat, mixed)):
            for half in range(2):
                at = (2 * i + half) * n
                out[s, at : at + n, :] = src[pl.ds(half * 4 + s, n, stride=8), :]
        out[s, 4 * n : 4 * n + 8, :] = tail


def finish(cell_count, arm, chi, back, field, new, volume):
    n = BX * BY
    here = arm[0]
    tail = jnp.sum(back[:, 4 * n : 4 * n + 8], axis=0)
    row = lax.broadcasted_iota(jnp.int32, (8, LANES), 0)
    chain = jnp.sum(jnp.where(row == 4, tail, 0.0), keepdims=True) / SPECIES
    field_sum = jnp.sum(jnp.where(row == here, tail, 0.0), keepdims=True)
    scale = cell_count / (SPECIES * STEPS * chain)
    chi_sum = chi[here, 0]
    for s in range(1, SPECIES):
        chi_sum = chi_sum + chi[here, s]
    mean_new = (1.0 - mixing) / cell_count * field_sum + mixing * chi_sum / SPECIES
    for q in range(SPECIES):
        for half in range(2):
            lanes = slice(half * LANES, (half + 1) * LANES)
            for x in range(BX):
                at = half * n + x * BY
                ys = slice(q * BY, (q + 1) * BY)
                volume[x, ys, lanes] = scale * back[q, at : at + BY, :]
                mixture = scale * back[q, 2 * n + at : 2 * n + at + BY, :]
                old = field[x, ys, lanes]
                new[x, ys, lanes] = old + mixing * (mixture - compress - old) - mean_new


def tiles(*lead):
    return jax.ShapeDtypeStruct(lead + (8, LANES), jnp.float32)


def scratch(*lead):
    return pltpu.VMEM(lead + (8, LANES), jnp.float32)


def call(kernel, outs, scratches=(), scalars=0, arrays=0):
    in_specs = [pl.BlockSpec(memory_space=pltpu.SMEM)] * scalars
    in_specs += [pl.BlockSpec(memory_space=pltpu.VMEM)] * arrays
    return pl.pallas_call(
        kernel,
        out_shape=outs,
        in_specs=in_specs,
        scratch_shapes=list(scratches),
        compiler_params=pltpu.CompilerParams(vmem_limit_bytes=VMEM_LIMIT),
    )


def local(fields, flory_chi):
    field_here = fields[0]
    arm = lax.axis_index("arm")[None]
    arms, size_gx, size_gy = (lax.axis_size(a) for a in ("arm", "gx", "gy"))
    cell_count = field_here.size * size_gx * size_gy
    n = BX * BY

    size = arms * size_gy
    at = lambda r: (r % arms) * size_gy + (r % size) // arms
    first_pairs = [(at(r), at(r ^ 1)) for r in range(size)]
    second_pairs = [(at(r), at(((r + 1) ^ 1) - 1)) for r in range(size)]

    def along_y(first, second):
        return (
            lax.ppermute(first, ("arm", "gy"), first_pairs),
            lax.ppermute(second, ("arm", "gy"), second_pairs),
        )

    def along_x(left, right):
        m = size_gx
        low = lax.ppermute(right, "gx", [(i, (i + 1) % m) for i in range(m)])
        high = lax.ppermute(left, "gx", [(i, (i - 1) % m) for i in range(m)])
        return low, high

    parts = size_gy // arms
    z_groups = [[y * parts + z for z in range(parts)] for y in range(size_gy // parts)]
    y_groups = [list(g) for g in zip(*z_groups)]

    def swap(spread, axis, groups=None):
        return lax.all_to_all(spread, axis, 0, 0, axis_index_groups=groups)

    payload = field_here.reshape(BX, arms, BY, 2, LANES).transpose(1, 3, 0, 2, 4)
    recv = lax.all_to_all(payload.reshape(arms, 2 * n, LANES), "arm", 0, 0)
    rows = tiles(BX, len(COEF_REACH))
    coef_flat, sums, e1, e2 = call(
        interleave_kernel,
        (jax.ShapeDtypeStruct((8 * n, LANES), jnp.float32), tiles(), rows, rows),
        scalars=1,
        arrays=1,
    )(arm, recv)
    coef_own = coef_flat.reshape(BX, BY, 8, LANES)
    y1, y2 = along_y(e1, e2)
    side = tiles(side_size(COEF_REACH))
    left, right = call(
        functools.partial(pack_sides, COEF_REACH), (side, side), scalars=1, arrays=3
    )(arm, coef_own, y1, y2)
    xlow, xhigh = along_x(left, right)

    own, wide_shape = tiles(BX, BY), tiles(BX + 8, BY)
    mid = tiles(packed_size(MID_REACH))
    coef, s2, s3, s4, e1, e2 = call(
        inner_first,
        (tiles(14 + BX, 6 + BY), own, own, wide_shape, mid, mid),
        [scratch(14 + BX, 6 + BY)] * 2,
        scalars=1,
        arrays=5,
    )(arm, coef_own, xlow, xhigh, y1, y2)
    y1, y2 = along_y(e1, e2)
    s5, s6, s7, s8, junction, spread = call(
        inner_second,
        (own,) * 5 + (tiles(size_gx),),
        [scratch(BX + 8, BY + 8)] * 2,
        scalars=1,
        arrays=5,
    )(arm, s4, y1, y2, coef, sums)

    y1, y2 = along_y(junction, junction)
    got = swap(spread, "gx")
    side = tiles(side_size(JUNC_REACH))
    left, right, spread = call(
        functools.partial(pack_sides, JUNC_REACH),
        (side, side, tiles(parts)),
        scalars=1,
        arrays=4,
    )(arm, junction, y1, y2, got)
    xlow, xhigh = along_x(left, right)
    got = swap(spread, "gy", z_groups)
    dens, wide, e1, e2, spread = call(
        outer_first,
        (own, wide_shape, mid, mid, tiles(len(z_groups))),
        [scratch(16 + BX, 8 + BY)] * 2,
        scalars=1,
        arrays=12,
    )(arm, junction, xlow, xhigh, y1, y2, coef, s4, s5, s6, s7, s8, got)
    y1, y2 = along_y(e1, e2)
    got = swap(spread, "gy", y_groups)
    out = call(
        outer_second,
        jax.ShapeDtypeStruct((arms, 4 * n + 8, LANES), jnp.float32),
        [scratch(BX + 8, BY + 8)] * 2 + [pltpu.VMEM((8 * n, LANES), jnp.float32)] * 2,
        scalars=2,
        arrays=8,
    )(arm, flory_chi, wide, y1, y2, coef, s2, s3, dens, got)

    back = lax.all_to_all(out, "arm", 0, 0)
    result = jax.ShapeDtypeStruct(field_here.shape, jnp.float32)
    field_out, volume = call(
        functools.partial(finish, cell_count), (result, result), scalars=2, arrays=2
    )(arm, flory_chi, back, field_here)
    return (field_out[None], volume[None])


def solution(mesh):
    placed = (P("arm", "gx", "gy", None), P())
    return jax.shard_map(
        local,
        mesh=mesh,
        in_specs=placed,
        out_specs=(P("arm", "gx", "gy", None), P("arm", "gx", "gy", None)),
        check_vma=False,
    )
```

```python
import functools

import jax
import jax.numpy as jnp
from jax import lax
from jax.experimental import pallas as pl
from jax.experimental.pallas import tpu as pltpu
from jax.sharding import PartitionSpec as P


SPECIES = 4
STEPS = 8


diffusion = 0.14
contour_step = 0.05
mixing = 0.5
compress = 1.0

LANES = 128
COEF_ONE = (1.0 - 6.0 * diffusion) / diffusion
COEF_FIELD = contour_step / diffusion
SCALE = diffusion**STEPS

BX, BY = 32, 4
VMEM_LIMIT = 16 * 1024 * 1024
COEF_REACH = (6, 5, 4)
MID_REACH = (3, 2, 1, 0)
JUNC_REACH = (7, 6, 5, 4)


def packed_size(reach):
    return sum(BX + 2 * r for r in reach)


def side_size(reach):
    return BY * (reach[0] + 1) + 2 * sum(reach)


def lane_masks():
    lane = lax.broadcasted_iota(jnp.int32, (8, LANES), 1)
    return lane == LANES - 1, lane == 0


def step(src, dst, coef, xs, ys, coef_shift):
    (x0, x1), (y0, y1) = xs, ys
    dx, dy = coef_shift
    last, first = lane_masks()
    v = src[x0:x1, y0:y1]
    other = pltpu.roll(v, 4, 2)
    up = pltpu.roll(jnp.where(last, other, v), 1, 3)
    down = pltpu.roll(jnp.where(first, other, v), LANES - 1, 3)
    total = (src[x0 - 1 : x1 - 1, y0:y1] + src[x0 + 1 : x1 + 1, y0:y1]) + (
        src[x0:x1, y0 - 1 : y1 - 1] + src[x0:x1, y0 + 1 : y1 + 1]
    )
    dst[x0:x1, y0:y1] = total + (up + down) + coef[x0 + dx : x1 + dx, y0 + dy : y1 + dy] * v


def interleave_kernel(arm, recv, coef, sums, first, second):
    n = BX * BY
    for s in range(SPECIES):
        for half in range(2):
            coef[pl.ds(half * 4 + s, n, stride=8), :] = (
                COEF_ONE - COEF_FIELD * recv[s, half * n : (half + 1) * n]
            )
        sums[s : s + 1, :] = jnp.sum(recv[s], axis=0, keepdims=True)
    sums[4:8, :] = jnp.zeros((4, LANES), jnp.float32)

    def body(up, down):
        cells = coef[...].reshape(BX, BY, 8, LANES)
        for j in range(len(COEF_REACH)):
            up[:, j] = cells[:, j]
            down[:, BY - 2 - j] = cells[:, BY - 1 - j]

    by_side(arm, first, second, body)


def by_side(arm, first, second, body):
    odd = arm[0] % 2

    @pl.when(odd == 0)
    def _():
        body(second, first)

    @pl.when(odd == 1)
    def _():
        body(first, second)


def pack_sides(reach, arm, own, first, second, *rest):
    if len(rest) == 4:
        got, left, right, total = rest
        total[...] = jnp.sum(got[...], axis=0)
    else:
        left, right = rest
    width, depth = reach[0] + 1, len(reach)

    def put(at, src, y, r):
        left[at : at + r] = src[0:r, y]
        right[at : at + r] = src[BX - r : BX, y]
        return at + r

    def body(low, high):
        at = 0
        for y in range(BY):
            at = put(at, own, y, width)
        for j, r in enumerate(reach):
            at = put(at, low, depth - 1 - j, r)
            at = put(at, high, j, r)

    by_side(arm, first, second, body)


def surround(arm, dst, reach, own, first, second, xlow, xhigh, shift):
    ox, oy = shift
    width, depth = reach[0] + 1, len(reach)
    dst[ox : ox + BX, oy : oy + BY] = own[...]

    def put(at, y, r):
        dst[ox - r : ox, y] = xlow[at : at + r]
        dst[ox + BX : ox + BX + r, y] = xhigh[at : at + r]
        return at + r

    at = 0
    for y in range(BY):
        at = put(at, oy + y, width)
    for j, r in enumerate(reach):
        at = put(at, oy - 1 - j, r)
        at = put(at, oy + BY + j, r)

    def body(low, high):
        dst[ox : ox + BX, oy - depth : oy] = low[...]
        dst[ox : ox + BX, oy + BY : oy + BY + depth] = high[...]

    by_side(arm, first, second, body)


def unpack(arm, dst, reach, first, second, shift):
    ox, oy = shift

    def body(low, high):
        offset = 0
        for j, r in enumerate(reach):
            n = BX + 2 * r
            dst[ox - r : ox + BX + r, oy - 1 - j] = low[offset : offset + n]
            dst[ox - r : ox + BX + r, oy + BY + j] = high[offset : offset + n]
            offset += n

    by_side(arm, first, second, body)


def emit(arm, src, shift, reach, wide, first, second):
    ox, oy = shift
    wide[...] = src[ox - 4 : ox + BX + 4, oy : oy + BY]

    def body(up, down):
        offset = 0
        for j, r in enumerate(reach):
            n = BX + 2 * r
            up[offset : offset + n] = src[ox - r : ox + BX + r, oy + j]
            down[offset : offset + n] = src[ox - r : ox + BX + r, oy + BY - 1 - j]
            offset += n

    by_side(arm, first, second, body)


def inner_first(arm, own, xlow, xhigh, y1, y2, coef, s2, s3, wide, e1, e2, a, b):
    surround(arm, coef, COEF_REACH, own, y1, y2, xlow, xhigh, (7, 3))
    here = (slice(7, 7 + BX), slice(3, 7))
    a[...] = 6.0 + coef[...]
    step(a, b, coef, (1, 45), (1, 9), (0, 0))
    s2[...] = b[here]
    step(b, a, coef, (2, 44), (2, 8), (0, 0))
    s3[...] = a[here]
    step(a, b, coef, (3, 43), (3, 7), (0, 0))
    emit(arm, b, (7, 3), MID_REACH, wide, e1, e2)


def others(v, shift):
    axis = v.ndim - 2
    row = lax.broadcasted_iota(jnp.int32, (8, LANES), 0) % 4
    return jnp.where(
        row + shift < 4, pltpu.roll(v, 8 - shift, axis), pltpu.roll(v, 4 - shift, axis)
    )


def inner_second(
    arm, wide, y1, y2, coef, sums, s5, s6, s7, s8, junction, spread, a, b
):
    a[0 : BX + 8, 4:8] = wide[...]
    unpack(arm, a, MID_REACH, y1, y2, (4, 4))
    here = (slice(4, 4 + BX), slice(4, 8))
    step(a, b, coef, (1, 39), (1, 11), (3, -1))
    s5[...] = b[here]
    step(b, a, coef, (2, 38), (2, 10), (3, -1))
    s6[...] = a[here]
    step(a, b, coef, (3, 37), (3, 9), (3, -1))
    s7[...] = b[here]
    step(b, a, coef, (4, 36), (4, 8), (3, -1))
    part = jnp.zeros((8, LANES), jnp.float32)
    for x in range(BX):
        q = a[x + 4, 4:8]
        s8[x] = q
        true = q * SCALE
        product = others(true, 1) * others(true, 2) * others(true, 3)
        junction[x] = product
        part = part + jnp.sum(q * product, axis=0)
    row = lax.broadcasted_iota(jnp.int32, (8, LANES), 0)
    chain = jnp.broadcast_to(jnp.sum(part, axis=0, keepdims=True), (8, LANES))
    spread[...] = jnp.broadcast_to(jnp.where(row == 4, chain, sums[...]), spread.shape)


def outer_first(
    arm, own, xlow, xhigh, y1, y2, coef, s4, s5, s6, s7, s8, total,
    dens, wide, e1, e2, spread, a, b
):
    spread[...] = jnp.broadcast_to(total[...], spread.shape)
    surround(arm, a, JUNC_REACH, own, y1, y2, xlow, xhigh, (8, 4))
    here = (slice(8, 8 + BX), slice(4, 8))
    shift = (-1, -1)
    step(a, b, coef, (1, 47), (1, 11), shift)
    dens[...] = 0.5 * s8[...] * own[...] + s7[...] * b[here]
    step(b, a, coef, (2, 46), (2, 10), shift)
    dens[...] += s6[...] * a[here]
    step(a, b, coef, (3, 45), (3, 9), shift)
    dens[...] += s5[...] * b[here]
    step(b, a, coef, (4, 44), (4, 8), shift)
    dens[...] += s4[4 : 4 + BX] * a[here]
    emit(arm, a, (8, 4), MID_REACH, wide, e1, e2)


def outer_second(
    arm, chi, wide, y1, y2, coef, s2, s3, dens, got, out, a, b, flat, mixed
):
    a[0 : BX + 8, 4:8] = wide[...]
    unpack(arm, a, MID_REACH, y1, y2, (4, 4))
    here = (slice(4, 4 + BX), slice(4, 8))
    rows = (8 * BX * BY, LANES)
    step(a, b, coef, (1, 39), (1, 11), (3, -1))
    flat[...] = (dens[...] + s3[...] * b[here]).reshape(rows)
    step(b, a, coef, (2, 38), (2, 10), (3, -1))
    flat[...] += (s2[...] * a[here]).reshape(rows)
    step(a, b, coef, (3, 37), (3, 9), (3, -1))
    flat[...] += ((6.0 + coef[7 : 7 + BX, 3:7]) * b[here]).reshape(rows)
    step(b, a, coef, (4, 36), (4, 8), (3, -1))
    d = flat[...].reshape(BX, BY, 8, LANES) + 0.5 * a[here]
    flat[...] = d.reshape(rows)
    row = lax.broadcasted_iota(jnp.int32, (8, LANES), 0) % 4
    total = None
    for k in range(SPECIES):
        weight = jnp.zeros((8, LANES), jnp.float32)
        for s in range(SPECIES):
            weight = jnp.where(row == s, chi[s, (s + k) % SPECIES] + compress, weight)
        term = weight * (others(d, k) if k else d)
        total = term if total is None else total + term
    mixed[...] = total.reshape(rows)
    n = BX * BY
    tail = jnp.sum(got[...], axis=0)
    for s in range(SPECIES):
        for i, src in enumerate((flat, mixed)):
            for half in range(2):
                at = (2 * i + half) * n
                out[s, at : at + n, :] = src[pl.ds(half * 4 + s, n, stride=8), :]
        out[s, 4 * n : 4 * n + 8, :] = tail


def finish(cell_count, arm, chi, back, field, new, volume):
    n = BX * BY
    here = arm[0]
    tail = jnp.sum(back[:, 4 * n : 4 * n + 8], axis=0)
    row = lax.broadcasted_iota(jnp.int32, (8, LANES), 0)
    chain = jnp.sum(jnp.where(row == 4, tail, 0.0), keepdims=True) / SPECIES
    field_sum = jnp.sum(jnp.where(row == here, tail, 0.0), keepdims=True)
    scale = cell_count / (SPECIES * STEPS * chain)
    chi_sum = chi[here, 0]
    for s in range(1, SPECIES):
        chi_sum = chi_sum + chi[here, s]
    mean_new = (1.0 - mixing) / cell_count * field_sum + mixing * chi_sum / SPECIES
    for q in range(SPECIES):
        for half in range(2):
            lanes = slice(half * LANES, (half + 1) * LANES)
            for x in range(BX):
                at = half * n + x * BY
                ys = slice(q * BY, (q + 1) * BY)
                volume[x, ys, lanes] = scale * back[q, at : at + BY, :]
                mixture = scale * back[q, 2 * n + at : 2 * n + at + BY, :]
                old = field[x, ys, lanes]
                new[x, ys, lanes] = old + mixing * (mixture - compress - old) - mean_new


def tiles(*lead):
    return jax.ShapeDtypeStruct(lead + (8, LANES), jnp.float32)


def scratch(*lead):
    return pltpu.VMEM(lead + (8, LANES), jnp.float32)


def call(kernel, outs, scratches=(), scalars=0, arrays=0):
    in_specs = [pl.BlockSpec(memory_space=pltpu.SMEM)] * scalars
    in_specs += [pl.BlockSpec(memory_space=pltpu.VMEM)] * arrays
    return pl.pallas_call(
        kernel,
        out_shape=outs,
        in_specs=in_specs,
        scratch_shapes=list(scratches),
        compiler_params=pltpu.CompilerParams(vmem_limit_bytes=VMEM_LIMIT),
    )


def local(fields, flory_chi):
    field_here = fields[0]
    arm = lax.axis_index("arm")[None]
    arms, size_gx, size_gy = (lax.axis_size(a) for a in ("arm", "gx", "gy"))
    cell_count = field_here.size * size_gx * size_gy
    n = BX * BY

    size = arms * size_gy
    at = lambda r: (r % arms) * size_gy + (r % size) // arms
    first_pairs = [(at(r), at(r ^ 1)) for r in range(size)]
    second_pairs = [(at(r), at(((r + 1) ^ 1) - 1)) for r in range(size)]

    def along_y(first, second):
        second = lax.ppermute(second, ("arm", "gy"), second_pairs)
        return lax.ppermute(first, ("arm", "gy"), first_pairs), second

    def along_x(left, right):
        m = size_gx
        low = lax.ppermute(right, "gx", [(i, (i + 1) % m) for i in range(m)])
        high = lax.ppermute(left, "gx", [(i, (i - 1) % m) for i in range(m)])
        return low, high

    parts = size_gy // arms
    z_groups = [[y * parts + z for z in range(parts)] for y in range(size_gy // parts)]
    y_groups = [list(g) for g in zip(*z_groups)]

    xy_groups = [
        [x * size_gy + g for x in range(size_gx) for g in group] for group in y_groups
    ]

    def swap(spread, axis, groups):
        return lax.all_to_all(spread, axis, 0, 0, axis_index_groups=groups)

    payload = field_here.reshape(BX, arms, BY, 2, LANES).transpose(1, 3, 0, 2, 4)
    recv = lax.all_to_all(payload.reshape(arms, 2 * n, LANES), "arm", 0, 0)
    rows = tiles(BX, len(COEF_REACH))
    coef_flat, sums, e1, e2 = call(
        interleave_kernel,
        (jax.ShapeDtypeStruct((8 * n, LANES), jnp.float32), tiles(), rows, rows),
        scalars=1,
        arrays=1,
    )(arm, recv)
    coef_own = coef_flat.reshape(BX, BY, 8, LANES)
    y1, y2 = along_y(e1, e2)
    side = tiles(side_size(COEF_REACH))
    left, right = call(
        functools.partial(pack_sides, COEF_REACH), (side, side), scalars=1, arrays=3
    )(arm, coef_own, y1, y2)
    xlow, xhigh = along_x(left, right)

    own, wide_shape = tiles(BX, BY), tiles(BX + 8, BY)
    mid = tiles(packed_size(MID_REACH))
    coef, s2, s3, s4, e1, e2 = call(
        inner_first,
        (tiles(14 + BX, 6 + BY), own, own, wide_shape, mid, mid),
        [scratch(14 + BX, 6 + BY)] * 2,
        scalars=1,
        arrays=5,
    )(arm, coef_own, xlow, xhigh, y1, y2)
    y1, y2 = along_y(e1, e2)
    s5, s6, s7, s8, junction, spread = call(
        inner_second,
        (own,) * 5 + (tiles(len(xy_groups[0])),),
        [scratch(BX + 8, BY + 8)] * 2,
        scalars=1,
        arrays=5,
    )(arm, s4, y1, y2, coef, sums)

    y1, y2 = along_y(junction, junction)
    got = swap(spread, ("gx", "gy"), xy_groups)
    side = tiles(side_size(JUNC_REACH))
    left, right, total = call(
        functools.partial(pack_sides, JUNC_REACH), (side, side, tiles()), scalars=1, arrays=4
    )(arm, junction, y1, y2, got)
    xlow, xhigh = along_x(left, right)
    dens, wide, e1, e2, spread = call(
        outer_first,
        (own, wide_shape, mid, mid, tiles(parts)),
        [scratch(16 + BX, 8 + BY)] * 2,
        scalars=1,
        arrays=12,
    )(arm, junction, xlow, xhigh, y1, y2, coef, s4, s5, s6, s7, s8, total)
    y1, y2 = along_y(e1, e2)
    got = swap(spread, "gy", z_groups)
    out = call(
        outer_second,
        jax.ShapeDtypeStruct((arms, 4 * n + 8, LANES), jnp.float32),
        [scratch(BX + 8, BY + 8)] * 2 + [pltpu.VMEM((8 * n, LANES), jnp.float32)] * 2,
        scalars=2,
        arrays=8,
    )(arm, flory_chi, wide, y1, y2, coef, s2, s3, dens, got)

    back = lax.all_to_all(out, "arm", 0, 0)
    result = jax.ShapeDtypeStruct(field_here.shape, jnp.float32)
    field_out, volume = call(
        functools.partial(finish, cell_count), (result, result), scalars=2, arrays=2
    )(arm, flory_chi, back, field_here)
    return (field_out[None], volume[None])


def solution(mesh):
    placed = (P("arm", "gx", "gy", None), P())
    return jax.shard_map(
        local,
        mesh=mesh,
        in_specs=placed,
        out_specs=(P("arm", "gx", "gy", None), P("arm", "gx", "gy", None)),
        check_vma=False,
    )
```

```python
import functools

import jax
import jax.numpy as jnp
from jax import lax
from jax.experimental import pallas as pl
from jax.experimental.pallas import tpu as pltpu
from jax.sharding import PartitionSpec as P


SPECIES = 4
STEPS = 8


diffusion = 0.14
contour_step = 0.05
mixing = 0.5
compress = 1.0

LANES = 128
COEF_ONE = (1.0 - 6.0 * diffusion) / diffusion
COEF_FIELD = contour_step / diffusion
SCALE = diffusion**STEPS

BX, BY = 32, 4
VMEM_LIMIT = 16 * 1024 * 1024
COEF_REACH = (6, 5, 4)
MID_REACH = (3, 2, 1, 0)
JUNC_REACH = (7, 6, 5, 4)


def packed_size(reach):
    return sum(BX + 2 * r for r in reach)


def side_size(reach):
    return BY * (reach[0] + 1) + 2 * sum(reach)


def lane_masks():
    lane = lax.broadcasted_iota(jnp.int32, (8, LANES), 1)
    return lane == LANES - 1, lane == 0


def step(src, dst, coef, origin, reach, depth, coef_shift):
    (ox, oy), (dx, dy) = origin, coef_shift
    last, first = lane_masks()
    for x in range(ox - reach, ox + BX + reach):
        outside = max(ox - x, x - (ox + BX - 1), 0)
        rows = min(depth, reach - outside)
        for y in range(oy - rows, oy + BY + rows):
            v = src[x, y]
            other = pltpu.roll(v, 4, 0)
            up = pltpu.roll(jnp.where(last, other, v), 1, 1)
            down = pltpu.roll(jnp.where(first, other, v), LANES - 1, 1)
            total = (src[x - 1, y] + src[x + 1, y]) + (src[x, y - 1] + src[x, y + 1])
            dst[x, y] = total + (up + down) + coef[x + dx, y + dy] * v


def spread_kernel(field, out):
    n = BX * BY
    for x in range(BX):
        for half in range(2):
            for q in range(SPECIES):
                at = half * n + x * BY
                out[q, at : at + BY, :] = field[
                    x, q * BY : (q + 1) * BY, half * LANES : (half + 1) * LANES
                ]


def interleave_kernel(arm, recv, coef, sums, first, second):
    n = BX * BY
    for s in range(SPECIES):
        for half in range(2):
            coef[pl.ds(half * 4 + s, n, stride=8), :] = (
                COEF_ONE - COEF_FIELD * recv[s, half * n : (half + 1) * n]
            )
        sums[s : s + 1, :] = jnp.sum(recv[s], axis=0, keepdims=True)
    sums[4:8, :] = jnp.zeros((4, LANES), jnp.float32)

    def body(up, down):
        cells = coef[...].reshape(BX, BY, 8, LANES)
        for j in range(len(COEF_REACH)):
            up[:, j] = cells[:, j]
            down[:, BY - 2 - j] = cells[:, BY - 1 - j]

    by_side(arm, first, second, body)


def by_side(arm, first, second, body):
    odd = arm[0] % 2

    @pl.when(odd == 0)
    def _():
        body(second, first)

    @pl.when(odd == 1)
    def _():
        body(first, second)


def pack_sides(reach, arm, own, first, second, *rest):
    if len(rest) == 4:
        got, left, right, total = rest
        total[...] = jnp.sum(got[...], axis=0)
    else:
        left, right = rest
    width, depth = reach[0] + 1, len(reach)

    def put(at, src, y, r):
        left[at : at + r] = src[0:r, y]
        right[at : at + r] = src[BX - r : BX, y]
        return at + r

    def body(low, high):
        at = 0
        for y in range(BY):
            at = put(at, own, y, width)
        for j, r in enumerate(reach):
            at = put(at, low, depth - 1 - j, r)
            at = put(at, high, j, r)

    by_side(arm, first, second, body)


def surround(arm, dst, reach, own, first, second, xlow, xhigh, shift):
    ox, oy = shift
    width, depth = reach[0] + 1, len(reach)
    dst[ox : ox + BX, oy : oy + BY] = own[...]

    def put(at, y, r):
        dst[ox - r : ox, y] = xlow[at : at + r]
        dst[ox + BX : ox + BX + r, y] = xhigh[at : at + r]
        return at + r

    at = 0
    for y in range(BY):
        at = put(at, oy + y, width)
    for j, r in enumerate(reach):
        at = put(at, oy - 1 - j, r)
        at = put(at, oy + BY + j, r)

    def body(low, high):
        dst[ox : ox + BX, oy - depth : oy] = low[...]
        dst[ox : ox + BX, oy + BY : oy + BY + depth] = high[...]

    by_side(arm, first, second, body)


def unpack(arm, dst, reach, first, second, shift):
    ox, oy = shift

    def body(low, high):
        offset = 0
        for j, r in enumerate(reach):
            n = BX + 2 * r
            dst[ox - r : ox + BX + r, oy - 1 - j] = low[offset : offset + n]
            dst[ox - r : ox + BX + r, oy + BY + j] = high[offset : offset + n]
            offset += n

    by_side(arm, first, second, body)


def emit(arm, src, shift, reach, wide, first, second):
    ox, oy = shift
    wide[...] = src[ox - 4 : ox + BX + 4, oy : oy + BY]

    def body(up, down):
        offset = 0
        for j, r in enumerate(reach):
            n = BX + 2 * r
            up[offset : offset + n] = src[ox - r : ox + BX + r, oy + j]
            down[offset : offset + n] = src[ox - r : ox + BX + r, oy + BY - 1 - j]
            offset += n

    by_side(arm, first, second, body)


def inner_first(arm, own, xlow, xhigh, y1, y2, coef, s2, s3, wide, e1, e2, a, b):
    surround(arm, coef, COEF_REACH, own, y1, y2, xlow, xhigh, (7, 3))
    here = (slice(7, 7 + BX), slice(3, 7))
    a[...] = 6.0 + coef[...]
    step(a, b, coef, (7, 3), 6, 2, (0, 0))
    s2[...] = b[here]
    step(b, a, coef, (7, 3), 5, 1, (0, 0))
    s3[...] = a[here]
    step(a, b, coef, (7, 3), 4, 0, (0, 0))
    emit(arm, b, (7, 3), MID_REACH, wide, e1, e2)


def others(v, shift):
    axis = v.ndim - 2
    row = lax.broadcasted_iota(jnp.int32, (8, LANES), 0) % 4
    return jnp.where(
        row + shift < 4, pltpu.roll(v, 8 - shift, axis), pltpu.roll(v, 4 - shift, axis)
    )


def inner_second(
    arm, wide, y1, y2, coef, sums, s5, s6, s7, s8, junction, spread, a, b
):
    a[0 : BX + 8, 4:8] = wide[...]
    unpack(arm, a, MID_REACH, y1, y2, (4, 4))
    here = (slice(4, 4 + BX), slice(4, 8))
    step(a, b, coef, (4, 4), 3, 3, (3, -1))
    s5[...] = b[here]
    step(b, a, coef, (4, 4), 2, 2, (3, -1))
    s6[...] = a[here]
    step(a, b, coef, (4, 4), 1, 1, (3, -1))
    s7[...] = b[here]
    step(b, a, coef, (4, 4), 0, 0, (3, -1))
    part = jnp.zeros((8, LANES), jnp.float32)
    for x in range(BX):
        q = a[x + 4, 4:8]
        s8[x] = q
        true = q * SCALE
        product = others(true, 1) * others(true, 2) * others(true, 3)
        junction[x] = product
        part = part + jnp.sum(q * product, axis=0)
    row = lax.broadcasted_iota(jnp.int32, (8, LANES), 0)
    chain = jnp.broadcast_to(jnp.sum(part, axis=0, keepdims=True), (8, LANES))
    spread[...] = jnp.broadcast_to(jnp.where(row == 4, chain, sums[...]), spread.shape)


def outer_first(
    arm, own, xlow, xhigh, y1, y2, coef, s4, s5, s6, s7, s8, total,
    dens, wide, e1, e2, spread, a, b
):
    spread[...] = jnp.broadcast_to(total[...], spread.shape)
    surround(arm, a, JUNC_REACH, own, y1, y2, xlow, xhigh, (8, 4))
    here = (slice(8, 8 + BX), slice(4, 8))
    shift = (-1, -1)
    step(a, b, coef, (8, 4), 7, 3, shift)
    dens[...] = 0.5 * s8[...] * own[...] + s7[...] * b[here]
    step(b, a, coef, (8, 4), 6, 2, shift)
    dens[...] += s6[...] * a[here]
    step(a, b, coef, (8, 4), 5, 1, shift)
    dens[...] += s5[...] * b[here]
    step(b, a, coef, (8, 4), 4, 0, shift)
    dens[...] += s4[4 : 4 + BX] * a[here]
    emit(arm, a, (8, 4), MID_REACH, wide, e1, e2)


def outer_second(
    arm, chi, wide, y1, y2, coef, s2, s3, dens, got, out, a, b, flat, mixed
):
    a[0 : BX + 8, 4:8] = wide[...]
    unpack(arm, a, MID_REACH, y1, y2, (4, 4))
    here = (slice(4, 4 + BX), slice(4, 8))
    rows = (8 * BX * BY, LANES)
    step(a, b, coef, (4, 4), 3, 3, (3, -1))
    flat[...] = (dens[...] + s3[...] * b[here]).reshape(rows)
    step(b, a, coef, (4, 4), 2, 2, (3, -1))
    flat[...] += (s2[...] * a[here]).reshape(rows)
    step(a, b, coef, (4, 4), 1, 1, (3, -1))
    flat[...] += ((6.0 + coef[7 : 7 + BX, 3:7]) * b[here]).reshape(rows)
    step(b, a, coef, (4, 4), 0, 0, (3, -1))
    d = flat[...].reshape(BX, BY, 8, LANES) + 0.5 * a[here]
    flat[...] = d.reshape(rows)
    row = lax.broadcasted_iota(jnp.int32, (8, LANES), 0) % 4
    total = None
    for k in range(SPECIES):
        weight = jnp.zeros((8, LANES), jnp.float32)
        for s in range(SPECIES):
            weight = jnp.where(row == s, chi[s, (s + k) % SPECIES] + compress, weight)
        term = weight * (others(d, k) if k else d)
        total = term if total is None else total + term
    mixed[...] = total.reshape(rows)
    n = BX * BY
    tail = jnp.sum(got[...], axis=0)
    for s in range(SPECIES):
        for i, src in enumerate((flat, mixed)):
            for half in range(2):
                at = (2 * i + half) * n
                out[s, at : at + n, :] = src[pl.ds(half * 4 + s, n, stride=8), :]
        out[s, 4 * n : 4 * n + 8, :] = tail


def finish(cell_count, arm, chi, back, field, new, volume):
    n = BX * BY
    here = arm[0]
    tail = jnp.sum(back[:, 4 * n : 4 * n + 8], axis=0)
    row = lax.broadcasted_iota(jnp.int32, (8, LANES), 0)
    chain = jnp.sum(jnp.where(row == 4, tail, 0.0), keepdims=True) / SPECIES
    field_sum = jnp.sum(jnp.where(row == here, tail, 0.0), keepdims=True)
    scale = cell_count / (SPECIES * STEPS * chain)
    chi_sum = chi[here, 0]
    for s in range(1, SPECIES):
        chi_sum = chi_sum + chi[here, s]
    mean_new = (1.0 - mixing) / cell_count * field_sum + mixing * chi_sum / SPECIES
    for q in range(SPECIES):
        for half in range(2):
            lanes = slice(half * LANES, (half + 1) * LANES)
            for x in range(BX):
                at = half * n + x * BY
                ys = slice(q * BY, (q + 1) * BY)
                volume[x, ys, lanes] = scale * back[q, at : at + BY, :]
                mixture = scale * back[q, 2 * n + at : 2 * n + at + BY, :]
                old = field[x, ys, lanes]
                new[x, ys, lanes] = old + mixing * (mixture - compress - old) - mean_new


def tiles(*lead):
    return jax.ShapeDtypeStruct(lead + (8, LANES), jnp.float32)


def scratch(*lead):
    return pltpu.VMEM(lead + (8, LANES), jnp.float32)


def call(kernel, outs, scratches=(), scalars=0, arrays=0):
    in_specs = [pl.BlockSpec(memory_space=pltpu.SMEM)] * scalars
    in_specs += [pl.BlockSpec(memory_space=pltpu.VMEM)] * arrays
    return pl.pallas_call(
        kernel,
        out_shape=outs,
        in_specs=in_specs,
        scratch_shapes=list(scratches),
        compiler_params=pltpu.CompilerParams(vmem_limit_bytes=VMEM_LIMIT),
    )


def local(fields, flory_chi):
    field_here = fields[0]
    arm = lax.axis_index("arm")[None]
    arms, size_gx, size_gy = (lax.axis_size(a) for a in ("arm", "gx", "gy"))
    cell_count = field_here.size * size_gx * size_gy
    n = BX * BY

    size = arms * size_gy
    at = lambda r: (r % arms) * size_gy + (r % size) // arms
    first_pairs = [(at(r), at(r ^ 1)) for r in range(size)]
    second_pairs = [(at(r), at(((r + 1) ^ 1) - 1)) for r in range(size)]

    def along_y(first, second):
        second = lax.ppermute(second, ("arm", "gy"), second_pairs)
        return lax.ppermute(first, ("arm", "gy"), first_pairs), second

    def along_x(left, right):
        m = size_gx
        low = lax.ppermute(right, "gx", [(i, (i + 1) % m) for i in range(m)])
        high = lax.ppermute(left, "gx", [(i, (i - 1) % m) for i in range(m)])
        return low, high

    parts = size_gy // arms
    z_groups = [[y * parts + z for z in range(parts)] for y in range(size_gy // parts)]
    y_groups = [list(g) for g in zip(*z_groups)]

    xy_groups = [
        [x * size_gy + g for x in range(size_gx) for g in group] for group in y_groups
    ]

    def swap(spread, axis, groups):
        return lax.all_to_all(spread, axis, 0, 0, axis_index_groups=groups)

    payload = call(
        spread_kernel, jax.ShapeDtypeStruct((arms, 2 * n, LANES), jnp.float32), arrays=1
    )(field_here)
    recv = lax.all_to_all(payload, "arm", 0, 0)
    rows = tiles(BX, len(COEF_REACH))
    coef_flat, sums, e1, e2 = call(
        interleave_kernel,
        (jax.ShapeDtypeStruct((8 * n, LANES), jnp.float32), tiles(), rows, rows),
        scalars=1,
        arrays=1,
    )(arm, recv)
    coef_own = coef_flat.reshape(BX, BY, 8, LANES)
    y1, y2 = along_y(e1, e2)
    side = tiles(side_size(COEF_REACH))
    left, right = call(
        functools.partial(pack_sides, COEF_REACH), (side, side), scalars=1, arrays=3
    )(arm, coef_own, y1, y2)
    xlow, xhigh = along_x(left, right)

    own, wide_shape = tiles(BX, BY), tiles(BX + 8, BY)
    mid = tiles(packed_size(MID_REACH))
    coef, s2, s3, s4, e1, e2 = call(
        inner_first,
        (tiles(14 + BX, 6 + BY), own, own, wide_shape, mid, mid),
        [scratch(14 + BX, 6 + BY)] * 2,
        scalars=1,
        arrays=5,
    )(arm, coef_own, xlow, xhigh, y1, y2)
    y1, y2 = along_y(e1, e2)
    s5, s6, s7, s8, junction, spread = call(
        inner_second,
        (own,) * 5 + (tiles(len(xy_groups[0])),),
        [scratch(BX + 8, BY + 8)] * 2,
        scalars=1,
        arrays=5,
    )(arm, s4, y1, y2, coef, sums)

    y1, y2 = along_y(junction, junction)
    got = swap(spread, ("gx", "gy"), xy_groups)
    side = tiles(side_size(JUNC_REACH))
    left, right, total = call(
        functools.partial(pack_sides, JUNC_REACH), (side, side, tiles()), scalars=1, arrays=4
    )(arm, junction, y1, y2, got)
    xlow, xhigh = along_x(left, right)
    dens, wide, e1, e2, spread = call(
        outer_first,
        (own, wide_shape, mid, mid, tiles(parts)),
        [scratch(16 + BX, 8 + BY)] * 2,
        scalars=1,
        arrays=12,
    )(arm, junction, xlow, xhigh, y1, y2, coef, s4, s5, s6, s7, s8, total)
    y1, y2 = along_y(e1, e2)
    got = swap(spread, "gy", z_groups)
    out = call(
        outer_second,
        jax.ShapeDtypeStruct((arms, 4 * n + 8, LANES), jnp.float32),
        [scratch(BX + 8, BY + 8)] * 2 + [pltpu.VMEM((8 * n, LANES), jnp.float32)] * 2,
        scalars=2,
        arrays=8,
    )(arm, flory_chi, wide, y1, y2, coef, s2, s3, dens, got)

    back = lax.all_to_all(out, "arm", 0, 0)
    result = jax.ShapeDtypeStruct(field_here.shape, jnp.float32)
    field_out, volume = call(
        functools.partial(finish, cell_count), (result, result), scalars=2, arrays=2
    )(arm, flory_chi, back, field_here)
    return (field_out[None], volume[None])


def solution(mesh):
    placed = (P("arm", "gx", "gy", None), P())
    return jax.shard_map(
        local,
        mesh=mesh,
        in_specs=placed,
        out_specs=(P("arm", "gx", "gy", None), P("arm", "gx", "gy", None)),
        check_vma=False,
    )
```

```python
import functools

import jax
import jax.numpy as jnp
from jax import lax
from jax.experimental import pallas as pl
from jax.experimental.pallas import tpu as pltpu
from jax.sharding import PartitionSpec as P


SPECIES = 4
STEPS = 8


diffusion = 0.14
contour_step = 0.05
mixing = 0.5
compress = 1.0

LANES = 128
COEF_ONE = (1.0 - 6.0 * diffusion) / diffusion
COEF_FIELD = contour_step / diffusion
SCALE = diffusion**STEPS

BX, BY = 32, 4
VMEM_LIMIT = 16 * 1024 * 1024
COEF_REACH = (6, 5, 4)
MID_REACH = (3, 2, 1, 0)
JUNC_REACH = (7, 6, 5, 4)


def packed_size(reach):
    return sum(BX + 2 * r for r in reach)


def side_size(reach):
    return BY * (reach[0] + 1) + 2 * sum(reach)


def lane_masks():
    lane = lax.broadcasted_iota(jnp.int32, (8, LANES), 1)
    return lane == LANES - 1, lane == 0


def step(src, dst, coef, origin, reach, depth, coef_shift):
    (ox, oy), (dx, dy) = origin, coef_shift
    last, first = lane_masks()
    for x in range(ox - reach, ox + BX + reach):
        outside = max(ox - x, x - (ox + BX - 1), 0)
        rows = min(depth, reach - outside)
        for y in range(oy - rows, oy + BY + rows):
            v = src[x, y]
            other = pltpu.roll(v, 4, 0)
            up = pltpu.roll(jnp.where(last, other, v), 1, 1)
            down = pltpu.roll(jnp.where(first, other, v), LANES - 1, 1)
            total = (src[x - 1, y] + src[x + 1, y]) + (src[x, y - 1] + src[x, y + 1])
            dst[x, y] = total + (up + down) + coef[x + dx, y + dy] * v


def spread_kernel(field, out):
    n = BX * BY
    for x in range(BX):
        for half in range(2):
            for q in range(SPECIES):
                at = half * n + x * BY
                out[q, at : at + BY, :] = field[
                    x, q * BY : (q + 1) * BY, half * LANES : (half + 1) * LANES
                ]


def interleave_kernel(arm, recv, coef, sums, left, right, first, second):
    n = BX * BY
    for s in range(SPECIES):
        for half in range(2):
            coef[pl.ds(half * 4 + s, n, stride=8), :] = (
                COEF_ONE - COEF_FIELD * recv[s, half * n : (half + 1) * n]
            )
        sums[s : s + 1, :] = jnp.sum(recv[s], axis=0, keepdims=True)
    sums[4:8, :] = jnp.zeros((4, LANES), jnp.float32)

    cells = coef[...].reshape(BX, BY, 8, LANES)
    width = left.shape[0]
    left[...] = cells[:width]
    right[...] = cells[BX - width :]

    def body(up, down):
        for j in range(len(COEF_REACH)):
            up[:, j] = cells[:, j]
            down[:, BY - 2 - j] = cells[:, BY - 1 - j]

    by_side(arm, first, second, body)


def by_side(arm, first, second, body):
    odd = arm[0] % 2

    @pl.when(odd == 0)
    def _():
        body(second, first)

    @pl.when(odd == 1)
    def _():
        body(first, second)


def pack_corners(reach, arm, low, high, first, second):
    width = low.shape[0]

    def body(up, down):
        at = 0
        for j, r in enumerate(reach):
            for dst, y in ((up, j), (down, BY - 1 - j)):
                dst[at : at + r] = low[width - r : width, y]
                dst[at + r : at + 2 * r] = high[0:r, y]
            at += 2 * r

    by_side(arm, first, second, body)


def pack_sides(reach, arm, own, first, second, got, left, right, total):
    total[...] = jnp.sum(got[...], axis=0)
    width, depth = reach[0] + 1, len(reach)

    def put(at, src, y, r):
        left[at : at + r] = src[0:r, y]
        right[at : at + r] = src[BX - r : BX, y]
        return at + r

    def body(low, high):
        at = 0
        for y in range(BY):
            at = put(at, own, y, width)
        for j, r in enumerate(reach):
            at = put(at, low, depth - 1 - j, r)
            at = put(at, high, j, r)

    by_side(arm, first, second, body)


def surround(arm, dst, reach, own, first, second, xlow, xhigh, shift):
    ox, oy = shift
    width, depth = reach[0] + 1, len(reach)
    dst[ox : ox + BX, oy : oy + BY] = own[...]

    def put(at, y, r):
        dst[ox - r : ox, y] = xlow[at : at + r]
        dst[ox + BX : ox + BX + r, y] = xhigh[at : at + r]
        return at + r

    at = 0
    for y in range(BY):
        at = put(at, oy + y, width)
    for j, r in enumerate(reach):
        at = put(at, oy - 1 - j, r)
        at = put(at, oy + BY + j, r)

    def body(low, high):
        dst[ox : ox + BX, oy - depth : oy] = low[...]
        dst[ox : ox + BX, oy + BY : oy + BY + depth] = high[...]

    by_side(arm, first, second, body)


def unpack(arm, dst, reach, first, second, shift):
    ox, oy = shift

    def body(low, high):
        offset = 0
        for j, r in enumerate(reach):
            n = BX + 2 * r
            dst[ox - r : ox + BX + r, oy - 1 - j] = low[offset : offset + n]
            dst[ox - r : ox + BX + r, oy + BY + j] = high[offset : offset + n]
            offset += n

    by_side(arm, first, second, body)


def emit(arm, src, shift, reach, wide, first, second):
    ox, oy = shift
    wide[...] = src[ox - 4 : ox + BX + 4, oy : oy + BY]

    def body(up, down):
        offset = 0
        for j, r in enumerate(reach):
            n = BX + 2 * r
            up[offset : offset + n] = src[ox - r : ox + BX + r, oy + j]
            down[offset : offset + n] = src[ox - r : ox + BX + r, oy + BY - 1 - j]
            offset += n

    by_side(arm, first, second, body)


def inner_first(
    arm, own, xlow, xhigh, y1, y2, c1, c2, coef, s2, s3, wide, e1, e2, a, b
):
    coef[0:7, 3:7] = xlow[...]
    coef[7 : 7 + BX, 3:7] = own[...]
    coef[7 + BX :, 3:7] = xhigh[...]

    def rows(low, high):
        coef[7 : 7 + BX, 0:3] = low[...]
        coef[7 : 7 + BX, 7:10] = high[...]

    def corners(low, high):
        at = 0
        for j, r in enumerate(COEF_REACH):
            for src, y in ((low, 2 - j), (high, 7 + j)):
                coef[7 - r : 7, y] = src[at : at + r]
                coef[7 + BX : 7 + BX + r, y] = src[at + r : at + 2 * r]
            at += 2 * r

    by_side(arm, y1, y2, rows)
    by_side(arm, c1, c2, corners)
    here = (slice(7, 7 + BX), slice(3, 7))
    a[...] = 6.0 + coef[...]
    step(a, b, coef, (7, 3), 6, 2, (0, 0))
    s2[...] = b[here]
    step(b, a, coef, (7, 3), 5, 1, (0, 0))
    s3[...] = a[here]
    step(a, b, coef, (7, 3), 4, 0, (0, 0))
    emit(arm, b, (7, 3), MID_REACH, wide, e1, e2)


def others(v, shift):
    axis = v.ndim - 2
    row = lax.broadcasted_iota(jnp.int32, (8, LANES), 0) % 4
    return jnp.where(
        row + shift < 4, pltpu.roll(v, 8 - shift, axis), pltpu.roll(v, 4 - shift, axis)
    )


def inner_second(
    arm, wide, y1, y2, coef, sums, s5, s6, s7, s8, junction, spread, a, b
):
    a[0 : BX + 8, 4:8] = wide[...]
    unpack(arm, a, MID_REACH, y1, y2, (4, 4))
    here = (slice(4, 4 + BX), slice(4, 8))
    step(a, b, coef, (4, 4), 3, 3, (3, -1))
    s5[...] = b[here]
    step(b, a, coef, (4, 4), 2, 2, (3, -1))
    s6[...] = a[here]
    step(a, b, coef, (4, 4), 1, 1, (3, -1))
    s7[...] = b[here]
    step(b, a, coef, (4, 4), 0, 0, (3, -1))
    part = jnp.zeros((8, LANES), jnp.float32)
    for x in range(BX):
        q = a[x + 4, 4:8]
        s8[x] = q
        true = q * SCALE
        product = others(true, 1) * others(true, 2) * others(true, 3)
        junction[x] = product
        part = part + jnp.sum(q * product, axis=0)
    row = lax.broadcasted_iota(jnp.int32, (8, LANES), 0)
    chain = jnp.broadcast_to(jnp.sum(part, axis=0, keepdims=True), (8, LANES))
    spread[...] = jnp.broadcast_to(jnp.where(row == 4, chain, sums[...]), spread.shape)


def outer_first(
    arm, own, xlow, xhigh, y1, y2, coef, s4, s5, s6, s7, s8, total, other,
    dens, wide, e1, e2, both, a, b
):
    both[...] = total[...] + other[...]
    surround(arm, a, JUNC_REACH, own, y1, y2, xlow, xhigh, (8, 4))
    here = (slice(8, 8 + BX), slice(4, 8))
    shift = (-1, -1)
    step(a, b, coef, (8, 4), 7, 3, shift)
    dens[...] = 0.5 * s8[...] * own[...] + s7[...] * b[here]
    step(b, a, coef, (8, 4), 6, 2, shift)
    dens[...] += s6[...] * a[here]
    step(a, b, coef, (8, 4), 5, 1, shift)
    dens[...] += s5[...] * b[here]
    step(b, a, coef, (8, 4), 4, 0, shift)
    dens[...] += s4[4 : 4 + BX] * a[here]
    emit(arm, a, (8, 4), MID_REACH, wide, e1, e2)


def outer_second(
    arm, chi, wide, y1, y2, coef, s2, s3, dens, total, other, out, a, b, flat, mixed
):
    a[0 : BX + 8, 4:8] = wide[...]
    unpack(arm, a, MID_REACH, y1, y2, (4, 4))
    here = (slice(4, 4 + BX), slice(4, 8))
    rows = (8 * BX * BY, LANES)
    step(a, b, coef, (4, 4), 3, 3, (3, -1))
    flat[...] = (dens[...] + s3[...] * b[here]).reshape(rows)
    step(b, a, coef, (4, 4), 2, 2, (3, -1))
    flat[...] += (s2[...] * a[here]).reshape(rows)
    step(a, b, coef, (4, 4), 1, 1, (3, -1))
    flat[...] += ((6.0 + coef[7 : 7 + BX, 3:7]) * b[here]).reshape(rows)
    step(b, a, coef, (4, 4), 0, 0, (3, -1))
    d = flat[...].reshape(BX, BY, 8, LANES) + 0.5 * a[here]
    flat[...] = d.reshape(rows)
    row = lax.broadcasted_iota(jnp.int32, (8, LANES), 0) % 4
    mixture = None
    for k in range(SPECIES):
        weight = jnp.zeros((8, LANES), jnp.float32)
        for s in range(SPECIES):
            weight = jnp.where(row == s, chi[s, (s + k) % SPECIES] + compress, weight)
        term = weight * (others(d, k) if k else d)
        mixture = term if mixture is None else mixture + term
    mixed[...] = mixture.reshape(rows)
    n = BX * BY
    tail = total[...] + other[...]
    for s in range(SPECIES):
        for i, src in enumerate((flat, mixed)):
            for half in range(2):
                at = (2 * i + half) * n
                out[s, at : at + n, :] = src[pl.ds(half * 4 + s, n, stride=8), :]
        out[s, 4 * n : 4 * n + 8, :] = tail


def finish(cell_count, arm, chi, back, field, new, volume):
    n = BX * BY
    here = arm[0]
    tail = jnp.sum(back[:, 4 * n : 4 * n + 8], axis=0)
    row = lax.broadcasted_iota(jnp.int32, (8, LANES), 0)
    chain = jnp.sum(jnp.where(row == 4, tail, 0.0), keepdims=True) / SPECIES
    field_sum = jnp.sum(jnp.where(row == here, tail, 0.0), keepdims=True)
    scale = cell_count / (SPECIES * STEPS * chain)
    chi_sum = chi[here, 0]
    for s in range(1, SPECIES):
        chi_sum = chi_sum + chi[here, s]
    mean_new = (1.0 - mixing) / cell_count * field_sum + mixing * chi_sum / SPECIES
    for q in range(SPECIES):
        for half in range(2):
            lanes = slice(half * LANES, (half + 1) * LANES)
            for x in range(BX):
                at = half * n + x * BY
                ys = slice(q * BY, (q + 1) * BY)
                volume[x, ys, lanes] = scale * back[q, at : at + BY, :]
                mixture = scale * back[q, 2 * n + at : 2 * n + at + BY, :]
                old = field[x, ys, lanes]
                new[x, ys, lanes] = old + mixing * (mixture - compress - old) - mean_new


def tiles(*lead):
    return jax.ShapeDtypeStruct(lead + (8, LANES), jnp.float32)


def scratch(*lead):
    return pltpu.VMEM(lead + (8, LANES), jnp.float32)


def call(kernel, outs, scratches=(), scalars=0, arrays=0):
    in_specs = [pl.BlockSpec(memory_space=pltpu.SMEM)] * scalars
    in_specs += [pl.BlockSpec(memory_space=pltpu.VMEM)] * arrays
    return pl.pallas_call(
        kernel,
        out_shape=outs,
        in_specs=in_specs,
        scratch_shapes=list(scratches),
        compiler_params=pltpu.CompilerParams(vmem_limit_bytes=VMEM_LIMIT),
    )


def local(fields, flory_chi):
    field_here = fields[0]
    arm = lax.axis_index("arm")[None]
    arms, size_gx, size_gy = (lax.axis_size(a) for a in ("arm", "gx", "gy"))
    cell_count = field_here.size * size_gx * size_gy
    n = BX * BY

    size = arms * size_gy
    at = lambda r: (r % arms) * size_gy + (r % size) // arms
    first_pairs = [(at(r), at(r ^ 1)) for r in range(size)]
    second_pairs = [(at(r), at(((r + 1) ^ 1) - 1)) for r in range(size)]

    def along_y(first, second):
        second = lax.ppermute(second, ("arm", "gy"), second_pairs)
        return lax.ppermute(first, ("arm", "gy"), first_pairs), second

    def along_x(left, right):
        m = size_gx
        low = lax.ppermute(right, "gx", [(i, (i + 1) % m) for i in range(m)])
        high = lax.ppermute(left, "gx", [(i, (i - 1) % m) for i in range(m)])
        return low, high

    parts = 4
    xy_groups = [
        [x * size_gy + g for x in range(size_gx) for g in range(z, size_gy, parts)]
        for z in range(parts)
    ]

    def along_z(tile, bit):
        return lax.ppermute(tile, "gy", [(i, i ^ bit) for i in range(size_gy)])

    payload = call(
        spread_kernel, jax.ShapeDtypeStruct((arms, 2 * n, LANES), jnp.float32), arrays=1
    )(field_here)
    recv = lax.all_to_all(payload, "arm", 0, 0)
    rows = tiles(BX, len(COEF_REACH))
    edge = tiles(COEF_REACH[0] + 1, BY)
    coef_flat, sums, left, right, e1, e2 = call(
        interleave_kernel,
        (jax.ShapeDtypeStruct((8 * n, LANES), jnp.float32), tiles(), edge, edge, rows, rows),
        scalars=1,
        arrays=1,
    )(arm, recv)
    coef_own = coef_flat.reshape(BX, BY, 8, LANES)
    corner = tiles(2 * sum(COEF_REACH))
    y1, y2 = along_y(e1, e2)
    xlow, xhigh = along_x(left, right)
    c1, c2 = call(
        functools.partial(pack_corners, COEF_REACH),
        (corner, corner),
        scalars=1,
        arrays=2,
    )(arm, xlow, xhigh)
    c1, c2 = along_y(c1, c2)

    own, wide_shape = tiles(BX, BY), tiles(BX + 8, BY)
    mid = tiles(packed_size(MID_REACH))
    coef, s2, s3, s4, e1, e2 = call(
        inner_first,
        (tiles(14 + BX, 6 + BY), own, own, wide_shape, mid, mid),
        [scratch(14 + BX, 6 + BY)] * 2,
        scalars=1,
        arrays=7,
    )(arm, coef_own, xlow, xhigh, y1, y2, c1, c2)
    y1, y2 = along_y(e1, e2)
    s5, s6, s7, s8, junction, spread = call(
        inner_second,
        (own,) * 5 + (tiles(len(xy_groups[0])),),
        [scratch(BX + 8, BY + 8)] * 2,
        scalars=1,
        arrays=5,
    )(arm, s4, y1, y2, coef, sums)

    y1, y2 = along_y(junction, junction)
    got = lax.all_to_all(spread, ("gx", "gy"), 0, 0, axis_index_groups=xy_groups)
    side = tiles(side_size(JUNC_REACH))
    left, right, total = call(
        functools.partial(pack_sides, JUNC_REACH),
        (side, side, tiles()),
        scalars=1,
        arrays=4,
    )(arm, junction, y1, y2, got)
    xlow, xhigh = along_x(left, right)
    other = along_z(total, 1)
    dens, wide, e1, e2, total = call(
        outer_first,
        (own, wide_shape, mid, mid, tiles()),
        [scratch(16 + BX, 8 + BY)] * 2,
        scalars=1,
        arrays=13,
    )(arm, junction, xlow, xhigh, y1, y2, coef, s4, s5, s6, s7, s8, total, other)
    y1, y2 = along_y(e1, e2)
    other = along_z(total, 2)
    out = call(
        outer_second,
        jax.ShapeDtypeStruct((arms, 4 * n + 8, LANES), jnp.float32),
        [scratch(BX + 8, BY + 8)] * 2 + [pltpu.VMEM((8 * n, LANES), jnp.float32)] * 2,
        scalars=2,
        arrays=9,
    )(arm, flory_chi, wide, y1, y2, coef, s2, s3, dens, total, other)

    back = lax.all_to_all(out, "arm", 0, 0)
    result = jax.ShapeDtypeStruct(field_here.shape, jnp.float32)
    field_out, volume = call(
        functools.partial(finish, cell_count), (result, result), scalars=2, arrays=2
    )(arm, flory_chi, back, field_here)
    return (field_out[None], volume[None])


def solution(mesh):
    placed = (P("arm", "gx", "gy", None), P())
    return jax.shard_map(
        local,
        mesh=mesh,
        in_specs=placed,
        out_specs=(P("arm", "gx", "gy", None), P("arm", "gx", "gy", None)),
        check_vma=False,
    )
```

```python
import functools

import jax
import jax.numpy as jnp
from jax import lax
from jax.experimental import pallas as pl
from jax.experimental.pallas import tpu as pltpu
from jax.sharding import PartitionSpec as P


SPECIES = 4
STEPS = 8


diffusion = 0.14
contour_step = 0.05
mixing = 0.5
compress = 1.0

LANES = 128
COEF_ONE = (1.0 - 6.0 * diffusion) / diffusion
COEF_FIELD = contour_step / diffusion
SCALE = diffusion**STEPS

BX, BY = 32, 4
VMEM_LIMIT = 16 * 1024 * 1024
COEF_REACH = (6, 5, 4)
MID_REACH = (3, 2, 1, 0)
JUNC_REACH = (7, 6, 5, 4)


def packed_size(reach):
    return sum(BX + 2 * r for r in reach)


def side_size(reach):
    return BY * (reach[0] + 1) + 2 * sum(reach)


def lane_masks():
    lane = lax.broadcasted_iota(jnp.int32, (8, LANES), 1)
    return lane == LANES - 1, lane == 0


def step(src, dst, coef, origin, reach, depth, coef_shift):
    (ox, oy), (dx, dy) = origin, coef_shift
    last, first = lane_masks()
    for x in range(ox - reach, ox + BX + reach):
        outside = max(ox - x, x - (ox + BX - 1), 0)
        rows = min(depth, reach - outside)
        for y in range(oy - rows, oy + BY + rows):
            v = src[x, y]
            other = pltpu.roll(v, 4, 0)
            up = pltpu.roll(jnp.where(last, other, v), 1, 1)
            down = pltpu.roll(jnp.where(first, other, v), LANES - 1, 1)
            total = (src[x - 1, y] + src[x + 1, y]) + (src[x, y - 1] + src[x, y + 1])
            dst[x, y] = total + (up + down) + coef[x + dx, y + dy] * v


def spread_kernel(field, out):
    n = BX * BY
    for x in range(BX):
        for half in range(2):
            for q in range(SPECIES):
                at = half * n + x * BY
                out[q, at : at + BY, :] = field[
                    x, q * BY : (q + 1) * BY, half * LANES : (half + 1) * LANES
                ]


def interleave_kernel(arm, recv, coef, sums, left, right, first, second):
    n = BX * BY
    for s in range(SPECIES):
        for half in range(2):
            coef[pl.ds(half * 4 + s, n, stride=8), :] = (
                COEF_ONE - COEF_FIELD * recv[s, half * n : (half + 1) * n]
            )
        sums[s : s + 1, :] = jnp.sum(recv[s], axis=0, keepdims=True)
    sums[4:8, :] = jnp.zeros((4, LANES), jnp.float32)

    cells = coef[...].reshape(BX, BY, 8, LANES)
    width = left.shape[0]
    left[...] = cells[:width]
    right[...] = cells[BX - width :]

    def body(up, down):
        for j in range(len(COEF_REACH)):
            up[:, j] = cells[:, j]
            down[:, BY - 2 - j] = cells[:, BY - 1 - j]

    by_side(arm, first, second, body)


def by_side(arm, first, second, body):
    odd = arm[0] % 2

    @pl.when(odd == 0)
    def _():
        body(second, first)

    @pl.when(odd == 1)
    def _():
        body(first, second)


def pack_corners(reach, arm, low, high, first, second):
    width = low.shape[0]

    def body(up, down):
        at = 0
        for j, r in enumerate(reach):
            for dst, y in ((up, j), (down, BY - 1 - j)):
                dst[at : at + r] = low[width - r : width, y]
                dst[at + r : at + 2 * r] = high[0:r, y]
            at += 2 * r

    by_side(arm, first, second, body)


def pack_sides(reach, arm, own, first, second, got, left, right, total):
    total[...] = jnp.sum(got[...], axis=0)
    width, depth = reach[0] + 1, len(reach)

    def put(at, src, y, r):
        left[at : at + r] = src[0:r, y]
        right[at : at + r] = src[BX - r : BX, y]
        return at + r

    def body(low, high):
        at = 0
        for y in range(BY):
            at = put(at, own, y, width)
        for j, r in enumerate(reach):
            at = put(at, low, depth - 1 - j, r)
            at = put(at, high, j, r)

    by_side(arm, first, second, body)


def surround(arm, dst, reach, own, first, second, xlow, xhigh, shift):
    ox, oy = shift
    width, depth = reach[0] + 1, len(reach)
    dst[ox : ox + BX, oy : oy + BY] = own[...]

    def put(at, y, r):
        dst[ox - r : ox, y] = xlow[at : at + r]
        dst[ox + BX : ox + BX + r, y] = xhigh[at : at + r]
        return at + r

    at = 0
    for y in range(BY):
        at = put(at, oy + y, width)
    for j, r in enumerate(reach):
        at = put(at, oy - 1 - j, r)
        at = put(at, oy + BY + j, r)

    def body(low, high):
        dst[ox : ox + BX, oy - depth : oy] = low[...]
        dst[ox : ox + BX, oy + BY : oy + BY + depth] = high[...]

    by_side(arm, first, second, body)


def unpack(arm, dst, reach, first, second, shift):
    ox, oy = shift

    def body(low, high):
        offset = 0
        for j, r in enumerate(reach):
            n = BX + 2 * r
            dst[ox - r : ox + BX + r, oy - 1 - j] = low[offset : offset + n]
            dst[ox - r : ox + BX + r, oy + BY + j] = high[offset : offset + n]
            offset += n

    by_side(arm, first, second, body)


def emit(arm, src, shift, reach, wide, first, second):
    ox, oy = shift
    wide[...] = src[ox - 4 : ox + BX + 4, oy : oy + BY]

    def body(up, down):
        offset = 0
        for j, r in enumerate(reach):
            n = BX + 2 * r
            up[offset : offset + n] = src[ox - r : ox + BX + r, oy + j]
            down[offset : offset + n] = src[ox - r : ox + BX + r, oy + BY - 1 - j]
            offset += n

    by_side(arm, first, second, body)


def inner_first(
    arm, own, xlow, xhigh, y1, y2, c1, c2, coef, s2, s3, wide, e1, e2, a, b
):
    coef[0:7, 3:7] = xlow[...]
    coef[7 : 7 + BX, 3:7] = own[...]
    coef[7 + BX :, 3:7] = xhigh[...]

    def rows(low, high):
        coef[7 : 7 + BX, 0:3] = low[...]
        coef[7 : 7 + BX, 7:10] = high[...]

    def corners(low, high):
        at = 0
        for j, r in enumerate(COEF_REACH):
            for src, y in ((low, 2 - j), (high, 7 + j)):
                coef[7 - r : 7, y] = src[at : at + r]
                coef[7 + BX : 7 + BX + r, y] = src[at + r : at + 2 * r]
            at += 2 * r

    by_side(arm, y1, y2, rows)
    by_side(arm, c1, c2, corners)
    here = (slice(7, 7 + BX), slice(3, 7))
    a[...] = 6.0 + coef[...]
    step(a, b, coef, (7, 3), 6, 2, (0, 0))
    s2[...] = b[here]
    step(b, a, coef, (7, 3), 5, 1, (0, 0))
    s3[...] = a[here]
    step(a, b, coef, (7, 3), 4, 0, (0, 0))
    emit(arm, b, (7, 3), MID_REACH, wide, e1, e2)


def others(v, shift):
    axis = v.ndim - 2
    row = lax.broadcasted_iota(jnp.int32, (8, LANES), 0) % 4
    return jnp.where(
        row + shift < 4, pltpu.roll(v, 8 - shift, axis), pltpu.roll(v, 4 - shift, axis)
    )


def inner_second(
    arm, wide, y1, y2, coef, sums, s5, s6, s7, s8, junction, spread, a, b
):
    a[0 : BX + 8, 4:8] = wide[...]
    unpack(arm, a, MID_REACH, y1, y2, (4, 4))
    here = (slice(4, 4 + BX), slice(4, 8))
    step(a, b, coef, (4, 4), 3, 3, (3, -1))
    s5[...] = b[here]
    step(b, a, coef, (4, 4), 2, 2, (3, -1))
    s6[...] = a[here]
    step(a, b, coef, (4, 4), 1, 1, (3, -1))
    s7[...] = b[here]
    step(b, a, coef, (4, 4), 0, 0, (3, -1))
    part = jnp.zeros((8, LANES), jnp.float32)
    for x in range(BX):
        q = a[x + 4, 4:8]
        s8[x] = q
        true = q * SCALE
        product = others(true, 1) * others(true, 2) * others(true, 3)
        junction[x] = product
        part = part + jnp.sum(q * product, axis=0)
    row = lax.broadcasted_iota(jnp.int32, (8, LANES), 0)
    chain = jnp.broadcast_to(jnp.sum(part, axis=0, keepdims=True), (8, LANES))
    spread[...] = jnp.broadcast_to(jnp.where(row == 4, chain, sums[...]), spread.shape)


def outer_first(
    arm, own, xlow, xhigh, y1, y2, coef, s4, s5, s6, s7, s8, total,
    dens, wide, e1, e2, kept, a, b
):
    kept[...] = total[...]
    surround(arm, a, JUNC_REACH, own, y1, y2, xlow, xhigh, (8, 4))
    here = (slice(8, 8 + BX), slice(4, 8))
    shift = (-1, -1)
    step(a, b, coef, (8, 4), 7, 3, shift)
    dens[...] = 0.5 * s8[...] * own[...] + s7[...] * b[here]
    step(b, a, coef, (8, 4), 6, 2, shift)
    dens[...] += s6[...] * a[here]
    step(a, b, coef, (8, 4), 5, 1, shift)
    dens[...] += s5[...] * b[here]
    step(b, a, coef, (8, 4), 4, 0, shift)
    dens[...] += s4[4 : 4 + BX] * a[here]
    emit(arm, a, (8, 4), MID_REACH, wide, e1, e2)


def outer_second(
    arm, chi, wide, y1, y2, coef, s2, s3, dens, total, other, out, a, b, flat, mixed
):
    a[0 : BX + 8, 4:8] = wide[...]
    unpack(arm, a, MID_REACH, y1, y2, (4, 4))
    here = (slice(4, 4 + BX), slice(4, 8))
    rows = (8 * BX * BY, LANES)
    step(a, b, coef, (4, 4), 3, 3, (3, -1))
    flat[...] = (dens[...] + s3[...] * b[here]).reshape(rows)
    step(b, a, coef, (4, 4), 2, 2, (3, -1))
    flat[...] += (s2[...] * a[here]).reshape(rows)
    step(a, b, coef, (4, 4), 1, 1, (3, -1))
    flat[...] += ((6.0 + coef[7 : 7 + BX, 3:7]) * b[here]).reshape(rows)
    step(b, a, coef, (4, 4), 0, 0, (3, -1))
    d = flat[...].reshape(BX, BY, 8, LANES) + 0.5 * a[here]
    flat[...] = d.reshape(rows)
    row = lax.broadcasted_iota(jnp.int32, (8, LANES), 0) % 4
    mixture = None
    for k in range(SPECIES):
        weight = jnp.zeros((8, LANES), jnp.float32)
        for s in range(SPECIES):
            weight = jnp.where(row == s, chi[s, (s + k) % SPECIES] + compress, weight)
        term = weight * (others(d, k) if k else d)
        mixture = term if mixture is None else mixture + term
    mixed[...] = mixture.reshape(rows)
    n = BX * BY
    tail = total[...] + other[...]
    for s in range(SPECIES):
        for i, src in enumerate((flat, mixed)):
            for half in range(2):
                at = (2 * i + half) * n
                out[s, at : at + n, :] = src[pl.ds(half * 4 + s, n, stride=8), :]
        out[s, 4 * n : 4 * n + 8, :] = tail


def finish(cell_count, arm, chi, back, field, new, volume):
    n = BX * BY
    here = arm[0]
    tail = jnp.sum(back[:, 4 * n : 4 * n + 8], axis=0)
    row = lax.broadcasted_iota(jnp.int32, (8, LANES), 0)
    chain = jnp.sum(jnp.where(row == 4, tail, 0.0), keepdims=True) / SPECIES
    field_sum = jnp.sum(jnp.where(row == here, tail, 0.0), keepdims=True)
    scale = cell_count / (SPECIES * STEPS * chain)
    chi_sum = chi[here, 0]
    for s in range(1, SPECIES):
        chi_sum = chi_sum + chi[here, s]
    mean_new = (1.0 - mixing) / cell_count * field_sum + mixing * chi_sum / SPECIES
    for q in range(SPECIES):
        for half in range(2):
            lanes = slice(half * LANES, (half + 1) * LANES)
            for x in range(BX):
                at = half * n + x * BY
                ys = slice(q * BY, (q + 1) * BY)
                volume[x, ys, lanes] = scale * back[q, at : at + BY, :]
                mixture = scale * back[q, 2 * n + at : 2 * n + at + BY, :]
                old = field[x, ys, lanes]
                new[x, ys, lanes] = old + mixing * (mixture - compress - old) - mean_new


def tiles(*lead):
    return jax.ShapeDtypeStruct(lead + (8, LANES), jnp.float32)


def scratch(*lead):
    return pltpu.VMEM(lead + (8, LANES), jnp.float32)


def call(kernel, outs, scratches=(), scalars=0, arrays=0):
    in_specs = [pl.BlockSpec(memory_space=pltpu.SMEM)] * scalars
    in_specs += [pl.BlockSpec(memory_space=pltpu.VMEM)] * arrays
    return pl.pallas_call(
        kernel,
        out_shape=outs,
        in_specs=in_specs,
        scratch_shapes=list(scratches),
        compiler_params=pltpu.CompilerParams(vmem_limit_bytes=VMEM_LIMIT),
    )


def local(fields, flory_chi):
    field_here = fields[0]
    arm = lax.axis_index("arm")[None]
    arms, size_gx, size_gy = (lax.axis_size(a) for a in ("arm", "gx", "gy"))
    cell_count = field_here.size * size_gx * size_gy
    n = BX * BY

    size = arms * size_gy
    at = lambda r: (r % arms) * size_gy + (r % size) // arms
    first_pairs = [(at(r), at(r ^ 1)) for r in range(size)]
    second_pairs = [(at(r), at(((r + 1) ^ 1) - 1)) for r in range(size)]

    def along_y(first, second):
        second = lax.ppermute(second, ("arm", "gy"), second_pairs)
        return lax.ppermute(first, ("arm", "gy"), first_pairs), second

    def along_x(left, right):
        m = size_gx
        low = lax.ppermute(right, "gx", [(i, (i + 1) % m) for i in range(m)])
        high = lax.ppermute(left, "gx", [(i, (i - 1) % m) for i in range(m)])
        return low, high

    parts = 4
    xy_groups = [
        [x * size_gy + g for x in range(size_gx) for g in range(z, size_gy, parts)]
        for z in range(parts)
    ]

    def along_z(tile, bit):
        return lax.ppermute(tile, "gy", [(i, i ^ bit) for i in range(size_gy)])

    payload = call(
        spread_kernel, jax.ShapeDtypeStruct((arms, 2 * n, LANES), jnp.float32), arrays=1
    )(field_here)
    recv = lax.all_to_all(payload, "arm", 0, 0)
    rows = tiles(BX, len(COEF_REACH))
    edge = tiles(COEF_REACH[0] + 1, BY)
    coef_flat, sums, left, right, e1, e2 = call(
        interleave_kernel,
        (jax.ShapeDtypeStruct((8 * n, LANES), jnp.float32), tiles(), edge, edge, rows, rows),
        scalars=1,
        arrays=1,
    )(arm, recv)
    coef_own = coef_flat.reshape(BX, BY, 8, LANES)
    corner = tiles(2 * sum(COEF_REACH))
    y1, y2 = along_y(e1, e2)
    xlow, xhigh = along_x(left, right)
    c1, c2 = call(
        functools.partial(pack_corners, COEF_REACH),
        (corner, corner),
        scalars=1,
        arrays=2,
    )(arm, xlow, xhigh)
    c1, c2 = along_y(c1, c2)

    own, wide_shape = tiles(BX, BY), tiles(BX + 8, BY)
    mid = tiles(packed_size(MID_REACH))
    coef, s2, s3, s4, e1, e2 = call(
        inner_first,
        (tiles(14 + BX, 6 + BY), own, own, wide_shape, mid, mid),
        [scratch(14 + BX, 6 + BY)] * 2,
        scalars=1,
        arrays=7,
    )(arm, coef_own, xlow, xhigh, y1, y2, c1, c2)
    y1, y2 = along_y(e1, e2)
    s5, s6, s7, s8, junction, spread = call(
        inner_second,
        (own,) * 5 + (tiles(len(xy_groups[0])),),
        [scratch(BX + 8, BY + 8)] * 2,
        scalars=1,
        arrays=5,
    )(arm, s4, y1, y2, coef, sums)

    y1, y2 = along_y(junction, junction)
    got = lax.all_to_all(spread, ("gx", "gy"), 0, 0, axis_index_groups=xy_groups)
    side = tiles(side_size(JUNC_REACH))
    left, right, total = call(
        functools.partial(pack_sides, JUNC_REACH),
        (side, side, tiles()),
        scalars=1,
        arrays=4,
    )(arm, junction, y1, y2, got)
    xlow, xhigh = along_x(left, right)
    other = along_z(total, 1)
    dens, wide, e1, e2, total = call(
        outer_first,
        (own, wide_shape, mid, mid, tiles()),
        [scratch(16 + BX, 8 + BY)] * 2,
        scalars=1,
        arrays=12,
    )(arm, junction, xlow, xhigh, y1, y2, coef, s4, s5, s6, s7, s8, total)
    y1, y2 = along_y(e1, e2)
    total = total + other
    other = along_z(total, 2)
    out = call(
        outer_second,
        jax.ShapeDtypeStruct((arms, 4 * n + 8, LANES), jnp.float32),
        [scratch(BX + 8, BY + 8)] * 2 + [pltpu.VMEM((8 * n, LANES), jnp.float32)] * 2,
        scalars=2,
        arrays=9,
    )(arm, flory_chi, wide, y1, y2, coef, s2, s3, dens, total, other)

    back = lax.all_to_all(out, "arm", 0, 0)
    result = jax.ShapeDtypeStruct(field_here.shape, jnp.float32)
    field_out, volume = call(
        functools.partial(finish, cell_count), (result, result), scalars=2, arrays=2
    )(arm, flory_chi, back, field_here)
    return (field_out[None], volume[None])


def solution(mesh):
    placed = (P("arm", "gx", "gy", None), P())
    return jax.shard_map(
        local,
        mesh=mesh,
        in_specs=placed,
        out_specs=(P("arm", "gx", "gy", None), P("arm", "gx", "gy", None)),
        check_vma=False,
    )
```

```python
import functools

import jax
import jax.numpy as jnp
from jax import lax
from jax.experimental import pallas as pl
from jax.experimental.pallas import tpu as pltpu
from jax.sharding import PartitionSpec as P


SPECIES = 4
STEPS = 8


diffusion = 0.14
contour_step = 0.05
mixing = 0.5
compress = 1.0

LANES = 128
COEF_ONE = (1.0 - 6.0 * diffusion) / diffusion
COEF_FIELD = contour_step / diffusion
SCALE = diffusion**STEPS

BX, BY = 32, 4
VMEM_LIMIT = 16 * 1024 * 1024
COEF_REACH = (6, 5, 4)
MID_REACH = (3, 2, 1, 0)
JUNC_REACH = (7, 6, 5, 4)


def packed_size(reach):
    return sum(BX + 2 * r for r in reach)


def side_size(reach):
    return BY * (reach[0] + 1) + 2 * sum(reach)


def lane_masks():
    lane = lax.broadcasted_iota(jnp.int32, (8, LANES), 1)
    return lane == LANES - 1, lane == 0


def lane_matrix():
    i = lax.broadcasted_iota(jnp.int32, (LANES, 2 * LANES), 0)
    j = lax.broadcasted_iota(jnp.int32, (LANES, 2 * LANES), 1)
    inside = (j < LANES) & ((i == j + 1) | (j == i + 1))
    across = ((i == LANES - 1) & (j == LANES)) | ((i == 0) & (j == 2 * LANES - 1))
    return jnp.where(inside | across, 1.0, 0.0).astype(jnp.bfloat16)


def lane_sums(column, matrix):
    n = column.shape[0]
    flat = column.reshape(n * 8, LANES)
    high = flat.astype(jnp.bfloat16)
    low = (flat - high.astype(jnp.float32)).astype(jnp.bfloat16)
    got = jnp.dot(high, matrix, preferred_element_type=jnp.float32)
    got = got + jnp.dot(low, matrix, preferred_element_type=jnp.float32)
    inside = got[:, :LANES].reshape(n, 8, LANES)
    across = got[:, LANES:].reshape(n, 8, LANES)
    return [inside[k] + pltpu.roll(across[k], 4, 0) for k in range(n)]


def step(src, dst, coef, origin, reach, depth, coef_shift):
    (ox, oy), (dx, dy) = origin, coef_shift
    last, first = lane_masks()
    matrix = lane_matrix()
    for x in range(ox - reach, ox + BX + reach):
        outside = max(ox - x, x - (ox + BX - 1), 0)
        rows = min(depth, reach - outside)
        y0, y1 = oy - rows, oy + BY + rows
        sums = lane_sums(src[x, y0:y1], matrix) if x % 3 == 0 else None
        for y in range(y0, y1):
            v = src[x, y]
            if sums is None:
                other = pltpu.roll(v, 4, 0)
                up = pltpu.roll(jnp.where(last, other, v), 1, 1)
                down = pltpu.roll(jnp.where(first, other, v), LANES - 1, 1)
                lanes = up + down
            else:
                lanes = sums[y - y0]
            total = (src[x - 1, y] + src[x + 1, y]) + (src[x, y - 1] + src[x, y + 1])
            dst[x, y] = total + lanes + coef[x + dx, y + dy] * v


def spread_kernel(field, out):
    n = BX * BY
    for x in range(BX):
        for half in range(2):
            for q in range(SPECIES):
                at = half * n + x * BY
                out[q, at : at + BY, :] = field[
                    x, q * BY : (q + 1) * BY, half * LANES : (half + 1) * LANES
                ]


def interleave_kernel(arm, recv, coef, sums, left, right, first, second):
    n = BX * BY
    for s in range(SPECIES):
        for half in range(2):
            coef[pl.ds(half * 4 + s, n, stride=8), :] = (
                COEF_ONE - COEF_FIELD * recv[s, half * n : (half + 1) * n]
            )
        sums[s : s + 1, :] = jnp.sum(recv[s], axis=0, keepdims=True)
    sums[4:8, :] = jnp.zeros((4, LANES), jnp.float32)

    cells = coef[...].reshape(BX, BY, 8, LANES)
    width = left.shape[0]
    left[...] = cells[:width]
    right[...] = cells[BX - width :]

    def body(up, down):
        for j in range(len(COEF_REACH)):
            up[:, j] = cells[:, j]
            down[:, BY - 2 - j] = cells[:, BY - 1 - j]

    by_side(arm, first, second, body)


def by_side(arm, first, second, body):
    odd = arm[0] % 2

    @pl.when(odd == 0)
    def _():
        body(second, first)

    @pl.when(odd == 1)
    def _():
        body(first, second)


def pack_corners(reach, arm, low, high, first, second):
    width = low.shape[0]

    def body(up, down):
        at = 0
        for j, r in enumerate(reach):
            for dst, y in ((up, j), (down, BY - 1 - j)):
                dst[at : at + r] = low[width - r : width, y]
                dst[at + r : at + 2 * r] = high[0:r, y]
            at += 2 * r

    by_side(arm, first, second, body)


def pack_sides(reach, arm, own, first, second, got, left, right, total):
    total[...] = jnp.sum(got[...], axis=0)
    width, depth = reach[0] + 1, len(reach)

    def put(at, src, y, r):
        left[at : at + r] = src[0:r, y]
        right[at : at + r] = src[BX - r : BX, y]
        return at + r

    def body(low, high):
        at = 0
        for y in range(BY):
            at = put(at, own, y, width)
        for j, r in enumerate(reach):
            at = put(at, low, depth - 1 - j, r)
            at = put(at, high, j, r)

    by_side(arm, first, second, body)


def surround(arm, dst, reach, own, first, second, xlow, xhigh, shift):
    ox, oy = shift
    width, depth = reach[0] + 1, len(reach)
    dst[ox : ox + BX, oy : oy + BY] = own[...]

    def put(at, y, r):
        dst[ox - r : ox, y] = xlow[at : at + r]
        dst[ox + BX : ox + BX + r, y] = xhigh[at : at + r]
        return at + r

    at = 0
    for y in range(BY):
        at = put(at, oy + y, width)
    for j, r in enumerate(reach):
        at = put(at, oy - 1 - j, r)
        at = put(at, oy + BY + j, r)

    def body(low, high):
        dst[ox : ox + BX, oy - depth : oy] = low[...]
        dst[ox : ox + BX, oy + BY : oy + BY + depth] = high[...]

    by_side(arm, first, second, body)


def unpack(arm, dst, reach, first, second, shift):
    ox, oy = shift

    def body(low, high):
        offset = 0
        for j, r in enumerate(reach):
            n = BX + 2 * r
            dst[ox - r : ox + BX + r, oy - 1 - j] = low[offset : offset + n]
            dst[ox - r : ox + BX + r, oy + BY + j] = high[offset : offset + n]
            offset += n

    by_side(arm, first, second, body)


def emit(arm, src, shift, reach, wide, first, second):
    ox, oy = shift
    wide[...] = src[ox - 4 : ox + BX + 4, oy : oy + BY]

    def body(up, down):
        offset = 0
        for j, r in enumerate(reach):
            n = BX + 2 * r
            up[offset : offset + n] = src[ox - r : ox + BX + r, oy + j]
            down[offset : offset + n] = src[ox - r : ox + BX + r, oy + BY - 1 - j]
            offset += n

    by_side(arm, first, second, body)


def inner_first(
    arm, own, xlow, xhigh, y1, y2, c1, c2, coef, s2, s3, wide, e1, e2, a, b
):
    coef[0:7, 3:7] = xlow[...]
    coef[7 : 7 + BX, 3:7] = own[...]
    coef[7 + BX :, 3:7] = xhigh[...]

    def rows(low, high):
        coef[7 : 7 + BX, 0:3] = low[...]
        coef[7 : 7 + BX, 7:10] = high[...]

    def corners(low, high):
        at = 0
        for j, r in enumerate(COEF_REACH):
            for src, y in ((low, 2 - j), (high, 7 + j)):
                coef[7 - r : 7, y] = src[at : at + r]
                coef[7 + BX : 7 + BX + r, y] = src[at + r : at + 2 * r]
            at += 2 * r

    by_side(arm, y1, y2, rows)
    by_side(arm, c1, c2, corners)
    here = (slice(7, 7 + BX), slice(3, 7))
    a[...] = 6.0 + coef[...]
    step(a, b, coef, (7, 3), 6, 2, (0, 0))
    s2[...] = b[here]
    step(b, a, coef, (7, 3), 5, 1, (0, 0))
    s3[...] = a[here]
    step(a, b, coef, (7, 3), 4, 0, (0, 0))
    emit(arm, b, (7, 3), MID_REACH, wide, e1, e2)


def others(v, shift):
    axis = v.ndim - 2
    row = lax.broadcasted_iota(jnp.int32, (8, LANES), 0) % 4
    return jnp.where(
        row + shift < 4, pltpu.roll(v, 8 - shift, axis), pltpu.roll(v, 4 - shift, axis)
    )


def inner_second(
    arm, wide, y1, y2, coef, sums, s5, s6, s7, s8, junction, spread, a, b
):
    a[0 : BX + 8, 4:8] = wide[...]
    unpack(arm, a, MID_REACH, y1, y2, (4, 4))
    here = (slice(4, 4 + BX), slice(4, 8))
    step(a, b, coef, (4, 4), 3, 3, (3, -1))
    s5[...] = b[here]
    step(b, a, coef, (4, 4), 2, 2, (3, -1))
    s6[...] = a[here]
    step(a, b, coef, (4, 4), 1, 1, (3, -1))
    s7[...] = b[here]
    step(b, a, coef, (4, 4), 0, 0, (3, -1))
    part = jnp.zeros((8, LANES), jnp.float32)
    for x in range(BX):
        q = a[x + 4, 4:8]
        s8[x] = q
        true = q * SCALE
        product = others(true, 1) * others(true, 2) * others(true, 3)
        junction[x] = product
        part = part + jnp.sum(q * product, axis=0)
    row = lax.broadcasted_iota(jnp.int32, (8, LANES), 0)
    chain = jnp.broadcast_to(jnp.sum(part, axis=0, keepdims=True), (8, LANES))
    spread[...] = jnp.broadcast_to(jnp.where(row == 4, chain, sums[...]), spread.shape)


def outer_first(
    arm, own, xlow, xhigh, y1, y2, coef, s4, s5, s6, s7, s8, total,
    dens, wide, e1, e2, kept, a, b
):
    kept[...] = total[...]
    surround(arm, a, JUNC_REACH, own, y1, y2, xlow, xhigh, (8, 4))
    here = (slice(8, 8 + BX), slice(4, 8))
    shift = (-1, -1)
    step(a, b, coef, (8, 4), 7, 3, shift)
    dens[...] = 0.5 * s8[...] * own[...] + s7[...] * b[here]
    step(b, a, coef, (8, 4), 6, 2, shift)
    dens[...] += s6[...] * a[here]
    step(a, b, coef, (8, 4), 5, 1, shift)
    dens[...] += s5[...] * b[here]
    step(b, a, coef, (8, 4), 4, 0, shift)
    dens[...] += s4[4 : 4 + BX] * a[here]
    emit(arm, a, (8, 4), MID_REACH, wide, e1, e2)


def outer_second(
    arm, chi, wide, y1, y2, coef, s2, s3, dens, out, a, b, flat, mixed
):
    a[0 : BX + 8, 4:8] = wide[...]
    unpack(arm, a, MID_REACH, y1, y2, (4, 4))
    here = (slice(4, 4 + BX), slice(4, 8))
    rows = (8 * BX * BY, LANES)
    step(a, b, coef, (4, 4), 3, 3, (3, -1))
    flat[...] = (dens[...] + s3[...] * b[here]).reshape(rows)
    step(b, a, coef, (4, 4), 2, 2, (3, -1))
    flat[...] += (s2[...] * a[here]).reshape(rows)
    step(a, b, coef, (4, 4), 1, 1, (3, -1))
    flat[...] += ((6.0 + coef[7 : 7 + BX, 3:7]) * b[here]).reshape(rows)
    step(b, a, coef, (4, 4), 0, 0, (3, -1))
    d = flat[...].reshape(BX, BY, 8, LANES) + 0.5 * a[here]
    flat[...] = d.reshape(rows)
    row = lax.broadcasted_iota(jnp.int32, (8, LANES), 0) % 4
    mixture = None
    for k in range(SPECIES):
        weight = jnp.zeros((8, LANES), jnp.float32)
        for s in range(SPECIES):
            weight = jnp.where(row == s, chi[s, (s + k) % SPECIES] + compress, weight)
        term = weight * (others(d, k) if k else d)
        mixture = term if mixture is None else mixture + term
    mixed[...] = mixture.reshape(rows)
    n = BX * BY
    for s in range(SPECIES):
        for i, src in enumerate((flat, mixed)):
            for half in range(2):
                at = (2 * i + half) * n
                out[s, at : at + n, :] = src[pl.ds(half * 4 + s, n, stride=8), :]


def finish(cell_count, arm, chi, back, field, new, volume):
    n = BX * BY
    here = arm[0]
    tail = jnp.sum(back[:, 4 * n : 4 * n + 8], axis=0)
    row = lax.broadcasted_iota(jnp.int32, (8, LANES), 0)
    chain = jnp.sum(jnp.where(row == 4, tail, 0.0), keepdims=True) / SPECIES
    field_sum = jnp.sum(jnp.where(row == here, tail, 0.0), keepdims=True)
    scale = cell_count / (SPECIES * STEPS * chain)
    chi_sum = chi[here, 0]
    for s in range(1, SPECIES):
        chi_sum = chi_sum + chi[here, s]
    mean_new = (1.0 - mixing) / cell_count * field_sum + mixing * chi_sum / SPECIES
    for q in range(SPECIES):
        for half in range(2):
            lanes = slice(half * LANES, (half + 1) * LANES)
            for x in range(BX):
                at = half * n + x * BY
                ys = slice(q * BY, (q + 1) * BY)
                volume[x, ys, lanes] = scale * back[q, at : at + BY, :]
                mixture = scale * back[q, 2 * n + at : 2 * n + at + BY, :]
                old = field[x, ys, lanes]
                new[x, ys, lanes] = old + mixing * (mixture - compress - old) - mean_new


def tiles(*lead):
    return jax.ShapeDtypeStruct(lead + (8, LANES), jnp.float32)


def scratch(*lead):
    return pltpu.VMEM(lead + (8, LANES), jnp.float32)


def call(kernel, outs, scratches=(), scalars=0, arrays=0):
    in_specs = [pl.BlockSpec(memory_space=pltpu.SMEM)] * scalars
    in_specs += [pl.BlockSpec(memory_space=pltpu.VMEM)] * arrays
    return pl.pallas_call(
        kernel,
        out_shape=outs,
        in_specs=in_specs,
        scratch_shapes=list(scratches),
        compiler_params=pltpu.CompilerParams(vmem_limit_bytes=VMEM_LIMIT),
    )


def local(fields, flory_chi):
    field_here = fields[0]
    arm = lax.axis_index("arm")[None]
    arms, size_gx, size_gy = (lax.axis_size(a) for a in ("arm", "gx", "gy"))
    cell_count = field_here.size * size_gx * size_gy
    n = BX * BY

    size = arms * size_gy
    at = lambda r: (r % arms) * size_gy + (r % size) // arms
    first_pairs = [(at(r), at(r ^ 1)) for r in range(size)]
    second_pairs = [(at(r), at(((r + 1) ^ 1) - 1)) for r in range(size)]

    def along_y(first, second):
        second = lax.ppermute(second, ("arm", "gy"), second_pairs)
        return lax.ppermute(first, ("arm", "gy"), first_pairs), second

    def along_x(left, right):
        m = size_gx
        low = lax.ppermute(right, "gx", [(i, (i + 1) % m) for i in range(m)])
        high = lax.ppermute(left, "gx", [(i, (i - 1) % m) for i in range(m)])
        return low, high

    parts = 4
    xy_groups = [
        [x * size_gy + g for x in range(size_gx) for g in range(z, size_gy, parts)]
        for z in range(parts)
    ]

    def along_z(tile, bit):
        return lax.ppermute(tile, "gy", [(i, i ^ bit) for i in range(size_gy)])

    payload = call(
        spread_kernel, jax.ShapeDtypeStruct((arms, 2 * n, LANES), jnp.float32), arrays=1
    )(field_here)
    recv = lax.all_to_all(payload, "arm", 0, 0)
    rows = tiles(BX, len(COEF_REACH))
    edge = tiles(COEF_REACH[0] + 1, BY)
    coef_flat, sums, left, right, e1, e2 = call(
        interleave_kernel,
        (jax.ShapeDtypeStruct((8 * n, LANES), jnp.float32), tiles(), edge, edge, rows, rows),
        scalars=1,
        arrays=1,
    )(arm, recv)
    coef_own = coef_flat.reshape(BX, BY, 8, LANES)
    corner = tiles(2 * sum(COEF_REACH))
    y1, y2 = along_y(e1, e2)
    xlow, xhigh = along_x(left, right)
    c1, c2 = call(
        functools.partial(pack_corners, COEF_REACH),
        (corner, corner),
        scalars=1,
        arrays=2,
    )(arm, xlow, xhigh)
    c1, c2 = along_y(c1, c2)

    own, wide_shape = tiles(BX, BY), tiles(BX + 8, BY)
    mid = tiles(packed_size(MID_REACH))
    coef, s2, s3, s4, e1, e2 = call(
        inner_first,
        (tiles(14 + BX, 6 + BY), own, own, wide_shape, mid, mid),
        [scratch(14 + BX, 6 + BY)] * 2,
        scalars=1,
        arrays=7,
    )(arm, coef_own, xlow, xhigh, y1, y2, c1, c2)
    y1, y2 = along_y(e1, e2)
    s5, s6, s7, s8, junction, spread = call(
        inner_second,
        (own,) * 5 + (tiles(len(xy_groups[0])),),
        [scratch(BX + 8, BY + 8)] * 2,
        scalars=1,
        arrays=5,
    )(arm, s4, y1, y2, coef, sums)

    y1, y2 = along_y(junction, junction)
    got = lax.all_to_all(spread, ("gx", "gy"), 0, 0, axis_index_groups=xy_groups)
    side = tiles(side_size(JUNC_REACH))
    left, right, total = call(
        functools.partial(pack_sides, JUNC_REACH),
        (side, side, tiles()),
        scalars=1,
        arrays=4,
    )(arm, junction, y1, y2, got)
    xlow, xhigh = along_x(left, right)
    other = along_z(total, 1)
    dens, wide, e1, e2, total = call(
        outer_first,
        (own, wide_shape, mid, mid, tiles()),
        [scratch(16 + BX, 8 + BY)] * 2,
        scalars=1,
        arrays=12,
    )(arm, junction, xlow, xhigh, y1, y2, coef, s4, s5, s6, s7, s8, total)
    y1, y2 = along_y(e1, e2)
    total = total + other
    other = along_z(total, 2)
    out = call(
        outer_second,
        jax.ShapeDtypeStruct((arms, 4 * n + 8, LANES), jnp.float32),
        [scratch(BX + 8, BY + 8)] * 2 + [pltpu.VMEM((8 * n, LANES), jnp.float32)] * 2,
        scalars=2,
        arrays=7,
    )(arm, flory_chi, wide, y1, y2, coef, s2, s3, dens)
    tail = jnp.broadcast_to(total + other, (arms, 8, LANES))
    out = lax.dynamic_update_slice(out, tail, (0, 4 * n, 0))

    back = lax.all_to_all(out, "arm", 0, 0)
    result = jax.ShapeDtypeStruct(field_here.shape, jnp.float32)
    field_out, volume = call(
        functools.partial(finish, cell_count), (result, result), scalars=2, arrays=2
    )(arm, flory_chi, back, field_here)
    return (field_out[None], volume[None])


def solution(mesh):
    placed = (P("arm", "gx", "gy", None), P())
    return jax.shard_map(
        local,
        mesh=mesh,
        in_specs=placed,
        out_specs=(P("arm", "gx", "gy", None), P("arm", "gx", "gy", None)),
        check_vma=False,
    )
```

```python
import functools

import jax
import jax.numpy as jnp
from jax import lax
from jax.experimental import pallas as pl
from jax.experimental.pallas import tpu as pltpu
from jax.sharding import PartitionSpec as P


SPECIES = 4
STEPS = 8


diffusion = 0.14
contour_step = 0.05
mixing = 0.5
compress = 1.0

LANES = 128
COEF_ONE = (1.0 - 6.0 * diffusion) / diffusion
COEF_FIELD = contour_step / diffusion
SCALE = diffusion**STEPS

BX, BY = 32, 4
VMEM_LIMIT = 16 * 1024 * 1024
COEF_REACH = (6, 5, 4)
MID_REACH = (3, 2, 1, 0)
JUNC_REACH = (7, 6, 5, 4)


def packed_size(reach):
    return sum(BX + 2 * r for r in reach)


def side_size(reach):
    return BY * (reach[0] + 1) + 2 * sum(reach)


def lane_masks():
    lane = lax.broadcasted_iota(jnp.int32, (8, LANES), 1)
    return lane == LANES - 1, lane == 0


def lane_matrix():
    i = lax.broadcasted_iota(jnp.int32, (LANES, 2 * LANES), 0)
    j = lax.broadcasted_iota(jnp.int32, (LANES, 2 * LANES), 1)
    inside = (j < LANES) & ((i == j + 1) | (j == i + 1))
    across = ((i == LANES - 1) & (j == LANES)) | ((i == 0) & (j == 2 * LANES - 1))
    return jnp.where(inside | across, 1.0, 0.0).astype(jnp.bfloat16)


def lane_sums(column, matrix):
    n = column.shape[0]
    flat = column.reshape(n * 8, LANES)
    high = flat.astype(jnp.bfloat16)
    low = (flat - high.astype(jnp.float32)).astype(jnp.bfloat16)
    got = jnp.dot(high, matrix, preferred_element_type=jnp.float32)
    got = got + jnp.dot(low, matrix, preferred_element_type=jnp.float32)
    inside = got[:, :LANES].reshape(n, 8, LANES)
    across = got[:, LANES:].reshape(n, 8, LANES)
    return [inside[k] + pltpu.roll(across[k], 4, 0) for k in range(n)]


def step(src, dst, coef, origin, reach, depth, coef_shift):
    (ox, oy), (dx, dy) = origin, coef_shift
    last, first = lane_masks()
    matrix = lane_matrix()
    for x in range(ox - reach, ox + BX + reach):
        outside = max(ox - x, x - (ox + BX - 1), 0)
        rows = min(depth, reach - outside)
        y0, y1 = oy - rows, oy + BY + rows
        sums = lane_sums(src[x, y0:y1], matrix) if x % 3 == 0 else None
        for y in range(y0, y1):
            v = src[x, y]
            if sums is None:
                other = pltpu.roll(v, 4, 0)
                up = pltpu.roll(jnp.where(last, other, v), 1, 1)
                down = pltpu.roll(jnp.where(first, other, v), LANES - 1, 1)
                lanes = up + down
            else:
                lanes = sums[y - y0]
            total = (src[x - 1, y] + src[x + 1, y]) + (src[x, y - 1] + src[x, y + 1])
            dst[x, y] = total + lanes + coef[x + dx, y + dy] * v


PARTS = 4
PART = BX // PARTS


def spread_kernel(field, out, held, sems):
    n = BX * BY
    copies = []
    for p in range(PARTS):
        part = pl.ds(p * PART, PART)
        copies.append(pltpu.make_async_copy(field.at[part], held.at[part], sems.at[p]))
        copies[p].start()
    for x in range(BX):
        if x % PART == 0:
            copies[x // PART].wait()
        for half in range(2):
            for q in range(SPECIES):
                at = half * n + x * BY
                out[q, at : at + BY, :] = held[
                    x, q * BY : (q + 1) * BY, half * LANES : (half + 1) * LANES
                ]


def interleave_kernel(arm, recv, coef, sums, left, right, first, second):
    n = BX * BY
    for s in range(SPECIES):
        for half in range(2):
            coef[pl.ds(half * 4 + s, n, stride=8), :] = (
                COEF_ONE - COEF_FIELD * recv[s, half * n : (half + 1) * n]
            )
        sums[s : s + 1, :] = jnp.sum(recv[s], axis=0, keepdims=True)
    sums[4:8, :] = jnp.zeros((4, LANES), jnp.float32)

    cells = coef[...].reshape(BX, BY, 8, LANES)
    width = left.shape[0]
    left[...] = cells[:width]
    right[...] = cells[BX - width :]

    def body(up, down):
        for j in range(len(COEF_REACH)):
            up[:, j] = cells[:, j]
            down[:, BY - 2 - j] = cells[:, BY - 1 - j]

    by_side(arm, first, second, body)


def by_side(arm, first, second, body):
    odd = arm[0] % 2

    @pl.when(odd == 0)
    def _():
        body(second, first)

    @pl.when(odd == 1)
    def _():
        body(first, second)


def pack_corners(reach, arm, low, high, first, second):
    width = low.shape[0]

    def body(up, down):
        at = 0
        for j, r in enumerate(reach):
            for dst, y in ((up, j), (down, BY - 1 - j)):
                dst[at : at + r] = low[width - r : width, y]
                dst[at + r : at + 2 * r] = high[0:r, y]
            at += 2 * r

    by_side(arm, first, second, body)


def pack_sides(reach, arm, own, first, second, got, left, right, total):
    total[...] = jnp.sum(got[...], axis=0)
    width, depth = reach[0] + 1, len(reach)

    def put(at, src, y, r):
        left[at : at + r] = src[0:r, y]
        right[at : at + r] = src[BX - r : BX, y]
        return at + r

    def body(low, high):
        at = 0
        for y in range(BY):
            at = put(at, own, y, width)
        for j, r in enumerate(reach):
            at = put(at, low, depth - 1 - j, r)
            at = put(at, high, j, r)

    by_side(arm, first, second, body)


def surround(arm, dst, reach, own, first, second, xlow, xhigh, shift):
    ox, oy = shift
    width, depth = reach[0] + 1, len(reach)
    dst[ox : ox + BX, oy : oy + BY] = own[...]

    def put(at, y, r):
        dst[ox - r : ox, y] = xlow[at : at + r]
        dst[ox + BX : ox + BX + r, y] = xhigh[at : at + r]
        return at + r

    at = 0
    for y in range(BY):
        at = put(at, oy + y, width)
    for j, r in enumerate(reach):
        at = put(at, oy - 1 - j, r)
        at = put(at, oy + BY + j, r)

    def body(low, high):
        dst[ox : ox + BX, oy - depth : oy] = low[...]
        dst[ox : ox + BX, oy + BY : oy + BY + depth] = high[...]

    by_side(arm, first, second, body)


def unpack(arm, dst, reach, first, second, shift):
    ox, oy = shift

    def body(low, high):
        offset = 0
        for j, r in enumerate(reach):
            n = BX + 2 * r
            dst[ox - r : ox + BX + r, oy - 1 - j] = low[offset : offset + n]
            dst[ox - r : ox + BX + r, oy + BY + j] = high[offset : offset + n]
            offset += n

    by_side(arm, first, second, body)


def emit(arm, src, shift, reach, wide, first, second):
    ox, oy = shift
    wide[...] = src[ox - 4 : ox + BX + 4, oy : oy + BY]

    def body(up, down):
        offset = 0
        for j, r in enumerate(reach):
            n = BX + 2 * r
            up[offset : offset + n] = src[ox - r : ox + BX + r, oy + j]
            down[offset : offset + n] = src[ox - r : ox + BX + r, oy + BY - 1 - j]
            offset += n

    by_side(arm, first, second, body)


def inner_first(
    arm, own, xlow, xhigh, y1, y2, c1, c2, coef, s2, s3, wide, e1, e2, a, b
):
    coef[0:7, 3:7] = xlow[...]
    coef[7 : 7 + BX, 3:7] = own[...]
    coef[7 + BX :, 3:7] = xhigh[...]

    def rows(low, high):
        coef[7 : 7 + BX, 0:3] = low[...]
        coef[7 : 7 + BX, 7:10] = high[...]

    def corners(low, high):
        at = 0
        for j, r in enumerate(COEF_REACH):
            for src, y in ((low, 2 - j), (high, 7 + j)):
                coef[7 - r : 7, y] = src[at : at + r]
                coef[7 + BX : 7 + BX + r, y] = src[at + r : at + 2 * r]
            at += 2 * r

    by_side(arm, y1, y2, rows)
    by_side(arm, c1, c2, corners)
    here = (slice(7, 7 + BX), slice(3, 7))
    a[...] = 6.0 + coef[...]
    step(a, b, coef, (7, 3), 6, 2, (0, 0))
    s2[...] = b[here]
    step(b, a, coef, (7, 3), 5, 1, (0, 0))
    s3[...] = a[here]
    step(a, b, coef, (7, 3), 4, 0, (0, 0))
    emit(arm, b, (7, 3), MID_REACH, wide, e1, e2)


def others(v, shift):
    axis = v.ndim - 2
    row = lax.broadcasted_iota(jnp.int32, (8, LANES), 0) % 4
    return jnp.where(
        row + shift < 4, pltpu.roll(v, 8 - shift, axis), pltpu.roll(v, 4 - shift, axis)
    )


def inner_second(
    arm, wide, y1, y2, coef, sums, s5, s6, s7, s8, junction, spread, a, b
):
    a[0 : BX + 8, 4:8] = wide[...]
    unpack(arm, a, MID_REACH, y1, y2, (4, 4))
    here = (slice(4, 4 + BX), slice(4, 8))
    step(a, b, coef, (4, 4), 3, 3, (3, -1))
    s5[...] = b[here]
    step(b, a, coef, (4, 4), 2, 2, (3, -1))
    s6[...] = a[here]
    step(a, b, coef, (4, 4), 1, 1, (3, -1))
    s7[...] = b[here]
    step(b, a, coef, (4, 4), 0, 0, (3, -1))
    part = jnp.zeros((8, LANES), jnp.float32)
    for x in range(BX):
        q = a[x + 4, 4:8]
        s8[x] = q
        true = q * SCALE
        product = others(true, 1) * others(true, 2) * others(true, 3)
        junction[x] = product
        part = part + jnp.sum(q * product, axis=0)
    row = lax.broadcasted_iota(jnp.int32, (8, LANES), 0)
    chain = jnp.broadcast_to(jnp.sum(part, axis=0, keepdims=True), (8, LANES))
    spread[...] = jnp.broadcast_to(jnp.where(row == 4, chain, sums[...]), spread.shape)


def outer_first(
    arm, own, xlow, xhigh, y1, y2, coef, s4, s5, s6, s7, s8, total,
    dens, wide, e1, e2, kept, a, b
):
    kept[...] = total[...]
    surround(arm, a, JUNC_REACH, own, y1, y2, xlow, xhigh, (8, 4))
    here = (slice(8, 8 + BX), slice(4, 8))
    shift = (-1, -1)
    step(a, b, coef, (8, 4), 7, 3, shift)
    dens[...] = 0.5 * s8[...] * own[...] + s7[...] * b[here]
    step(b, a, coef, (8, 4), 6, 2, shift)
    dens[...] += s6[...] * a[here]
    step(a, b, coef, (8, 4), 5, 1, shift)
    dens[...] += s5[...] * b[here]
    step(b, a, coef, (8, 4), 4, 0, shift)
    dens[...] += s4[4 : 4 + BX] * a[here]
    emit(arm, a, (8, 4), MID_REACH, wide, e1, e2)


def outer_second(
    arm, chi, wide, y1, y2, coef, s2, s3, dens, out, a, b, flat, mixed
):
    a[0 : BX + 8, 4:8] = wide[...]
    unpack(arm, a, MID_REACH, y1, y2, (4, 4))
    here = (slice(4, 4 + BX), slice(4, 8))
    rows = (8 * BX * BY, LANES)
    step(a, b, coef, (4, 4), 3, 3, (3, -1))
    flat[...] = (dens[...] + s3[...] * b[here]).reshape(rows)
    step(b, a, coef, (4, 4), 2, 2, (3, -1))
    flat[...] += (s2[...] * a[here]).reshape(rows)
    step(a, b, coef, (4, 4), 1, 1, (3, -1))
    flat[...] += ((6.0 + coef[7 : 7 + BX, 3:7]) * b[here]).reshape(rows)
    step(b, a, coef, (4, 4), 0, 0, (3, -1))
    d = flat[...].reshape(BX, BY, 8, LANES) + 0.5 * a[here]
    flat[...] = d.reshape(rows)
    row = lax.broadcasted_iota(jnp.int32, (8, LANES), 0) % 4
    mixture = None
    for k in range(SPECIES):
        weight = jnp.zeros((8, LANES), jnp.float32)
        for s in range(SPECIES):
            weight = jnp.where(row == s, chi[s, (s + k) % SPECIES] + compress, weight)
        term = weight * (others(d, k) if k else d)
        mixture = term if mixture is None else mixture + term
    mixed[...] = mixture.reshape(rows)
    n = BX * BY
    for s in range(SPECIES):
        for i, src in enumerate((flat, mixed)):
            for half in range(2):
                at = (2 * i + half) * n
                out[s, at : at + n, :] = src[pl.ds(half * 4 + s, n, stride=8), :]


def finish(cell_count, arm, chi, back, field, new_out, volume_out, new, volume, sems):
    n = BX * BY
    here = arm[0]
    tail = jnp.sum(back[:, 4 * n : 4 * n + 8], axis=0)
    row = lax.broadcasted_iota(jnp.int32, (8, LANES), 0)
    chain = jnp.sum(jnp.where(row == 4, tail, 0.0), keepdims=True) / SPECIES
    field_sum = jnp.sum(jnp.where(row == here, tail, 0.0), keepdims=True)
    scale = cell_count / (SPECIES * STEPS * chain)
    chi_sum = chi[here, 0]
    for s in range(1, SPECIES):
        chi_sum = chi_sum + chi[here, s]
    mean_new = (1.0 - mixing) / cell_count * field_sum + mixing * chi_sum / SPECIES
    copies = []
    for p in range(PARTS):
        for q in range(SPECIES):
            for half in range(2):
                lanes = slice(half * LANES, (half + 1) * LANES)
                for x in range(p * PART, (p + 1) * PART):
                    at = half * n + x * BY
                    ys = slice(q * BY, (q + 1) * BY)
                    volume[x, ys, lanes] = scale * back[q, at : at + BY, :]
                    mixture = scale * back[q, 2 * n + at : 2 * n + at + BY, :]
                    old = field[x, ys, lanes]
                    new[x, ys, lanes] = (
                        old + mixing * (mixture - compress - old) - mean_new
                    )
        part = pl.ds(p * PART, PART)
        for i, (src, dst) in enumerate(((volume, volume_out), (new, new_out))):
            copy = pltpu.make_async_copy(src.at[part], dst.at[part], sems.at[i, p])
            copy.start()
            copies.append(copy)
    for copy in copies:
        copy.wait()


def tiles(*lead):
    return jax.ShapeDtypeStruct(lead + (8, LANES), jnp.float32)


def scratch(*lead):
    return pltpu.VMEM(lead + (8, LANES), jnp.float32)


def call(kernel, outs, scratches=(), scalars=0, arrays=0):
    in_specs = [pl.BlockSpec(memory_space=pltpu.SMEM)] * scalars
    in_specs += [pl.BlockSpec(memory_space=pltpu.VMEM)] * arrays
    return pl.pallas_call(
        kernel,
        out_shape=outs,
        in_specs=in_specs,
        scratch_shapes=list(scratches),
        compiler_params=pltpu.CompilerParams(vmem_limit_bytes=VMEM_LIMIT),
    )


def local(fields, flory_chi):
    field_here = fields[0]
    arm = lax.axis_index("arm")[None]
    arms, size_gx, size_gy = (lax.axis_size(a) for a in ("arm", "gx", "gy"))
    cell_count = field_here.size * size_gx * size_gy
    n = BX * BY

    size = arms * size_gy
    at = lambda r: (r % arms) * size_gy + (r % size) // arms
    first_pairs = [(at(r), at(r ^ 1)) for r in range(size)]
    second_pairs = [(at(r), at(((r + 1) ^ 1) - 1)) for r in range(size)]

    def along_y(first, second):
        second = lax.ppermute(second, ("arm", "gy"), second_pairs)
        return lax.ppermute(first, ("arm", "gy"), first_pairs), second

    def along_x(left, right):
        m = size_gx
        low = lax.ppermute(right, "gx", [(i, (i + 1) % m) for i in range(m)])
        high = lax.ppermute(left, "gx", [(i, (i - 1) % m) for i in range(m)])
        return low, high

    parts = 4
    xy_groups = [
        [x * size_gy + g for x in range(size_gx) for g in range(z, size_gy, parts)]
        for z in range(parts)
    ]

    def along_z(tile, bit):
        return lax.ppermute(tile, "gy", [(i, i ^ bit) for i in range(size_gy)])

    block = pltpu.VMEM(field_here.shape, jnp.float32)
    in_hbm = pl.BlockSpec(memory_space=pltpu.HBM)
    payload = pl.pallas_call(
        spread_kernel,
        out_shape=jax.ShapeDtypeStruct((arms, 2 * n, LANES), jnp.float32),
        in_specs=[in_hbm],
        scratch_shapes=[block, pltpu.SemaphoreType.DMA((PARTS,))],
        compiler_params=pltpu.CompilerParams(vmem_limit_bytes=60 * 1024 * 1024),
    )(field_here)
    recv = lax.all_to_all(payload, "arm", 0, 0)
    rows = tiles(BX, len(COEF_REACH))
    edge = tiles(COEF_REACH[0] + 1, BY)
    coef_flat, sums, left, right, e1, e2 = call(
        interleave_kernel,
        (jax.ShapeDtypeStruct((8 * n, LANES), jnp.float32), tiles(), edge, edge, rows, rows),
        scalars=1,
        arrays=1,
    )(arm, recv)
    coef_own = coef_flat.reshape(BX, BY, 8, LANES)
    corner = tiles(2 * sum(COEF_REACH))
    y1, y2 = along_y(e1, e2)
    xlow, xhigh = along_x(left, right)
    c1, c2 = call(
        functools.partial(pack_corners, COEF_REACH),
        (corner, corner),
        scalars=1,
        arrays=2,
    )(arm, xlow, xhigh)
    c1, c2 = along_y(c1, c2)

    own, wide_shape = tiles(BX, BY), tiles(BX + 8, BY)
    mid = tiles(packed_size(MID_REACH))
    coef, s2, s3, s4, e1, e2 = call(
        inner_first,
        (tiles(14 + BX, 6 + BY), own, own, wide_shape, mid, mid),
        [scratch(14 + BX, 6 + BY)] * 2,
        scalars=1,
        arrays=7,
    )(arm, coef_own, xlow, xhigh, y1, y2, c1, c2)
    y1, y2 = along_y(e1, e2)
    s5, s6, s7, s8, junction, spread = call(
        inner_second,
        (own,) * 5 + (tiles(len(xy_groups[0])),),
        [scratch(BX + 8, BY + 8)] * 2,
        scalars=1,
        arrays=5,
    )(arm, s4, y1, y2, coef, sums)

    y1, y2 = along_y(junction, junction)
    got = lax.all_to_all(spread, ("gx", "gy"), 0, 0, axis_index_groups=xy_groups)
    side = tiles(side_size(JUNC_REACH))
    left, right, total = call(
        functools.partial(pack_sides, JUNC_REACH),
        (side, side, tiles()),
        scalars=1,
        arrays=4,
    )(arm, junction, y1, y2, got)
    xlow, xhigh = along_x(left, right)
    other = along_z(total, 1)
    dens, wide, e1, e2, total = call(
        outer_first,
        (own, wide_shape, mid, mid, tiles()),
        [scratch(16 + BX, 8 + BY)] * 2,
        scalars=1,
        arrays=12,
    )(arm, junction, xlow, xhigh, y1, y2, coef, s4, s5, s6, s7, s8, total)
    y1, y2 = along_y(e1, e2)
    total = total + other
    other = along_z(total, 2)
    out = call(
        outer_second,
        jax.ShapeDtypeStruct((arms, 4 * n + 8, LANES), jnp.float32),
        [scratch(BX + 8, BY + 8)] * 2 + [pltpu.VMEM((8 * n, LANES), jnp.float32)] * 2,
        scalars=2,
        arrays=7,
    )(arm, flory_chi, wide, y1, y2, coef, s2, s3, dens)
    tail = jnp.broadcast_to(total + other, (arms, 8, LANES))
    out = lax.dynamic_update_slice(out, tail, (0, 4 * n, 0))

    back = lax.all_to_all(out, "arm", 0, 0)
    result = jax.ShapeDtypeStruct(field_here.shape, jnp.float32)
    field_out, volume = pl.pallas_call(
        functools.partial(finish, cell_count),
        out_shape=(result, result),
        in_specs=[pl.BlockSpec(memory_space=pltpu.SMEM)] * 2
        + [pl.BlockSpec(memory_space=pltpu.VMEM)] * 2,
        out_specs=(in_hbm, in_hbm),
        scratch_shapes=[block, block, pltpu.SemaphoreType.DMA((2, PARTS))],
        compiler_params=pltpu.CompilerParams(vmem_limit_bytes=VMEM_LIMIT),
    )(arm, flory_chi, back, field_here)
    return (field_out[None], volume[None])


def solution(mesh):
    placed = (P("arm", "gx", "gy", None), P())
    return jax.shard_map(
        local,
        mesh=mesh,
        in_specs=placed,
        out_specs=(P("arm", "gx", "gy", None), P("arm", "gx", "gy", None)),
        check_vma=False,
    )
```
